32 devices in a mesh: group: 2 (over y), lender: 4 (over z), tensor: 4 (over x, core).
Axes of the slice: x: 2, y: 2, z: 4, core: 2. Of those that a mesh axis runs over, the one named last changes fastest.
Arguments:
- activations: bfloat16 [16, 8192], P('group', 'lender'), parts along dimension 0, may hold values from -400 to 400
- norm_gain: bfloat16 [8192], P('lender'), may hold values from 0.099609375 to 1.8984375
- w_query: bfloat16 [8192, 8192], P('lender', 'tensor'), may hold values from -0.0625 to 0.0625
- w_out: bfloat16 [8192, 8192], P('tensor', 'lender'), may hold values from -0.0625 to 0.0625
- key_pool: bfloat16 [8, 256, 128, 128], P('tensor', ('group', 'lender')), parts along dimension 1, may hold values from -800 to 800
- value_block_store: bfloat16 [8, 256, 128, 128], P('tensor', ('group', 'lender')), parts along dimension 1, may hold values from -48 to 48
- block_list: int32 [16, 8, 16], P('group', 'tensor'), parts along dimension 0, may hold values from 0 to 127, as said below
- block_slot_table: int32 [8, 256], P('tensor', 'group'), parts along dimension 1, may hold values from 0 to 127, each once within a row
- kept_len: int32 [16, 8], P('group', 'tensor'), parts along dimension 0, may hold values from 1 to 16, as said below
Outputs:
- output: bfloat16 [16, 8192], P(('group', 'tensor'), 'lender'), parts along dimension 0
The draws below stay inside these ranges and needn't reach their ends.
There are 2 independent parts, one for each index of `group`. The reference program is written for one: setup_inputs(seed, part) draws one part's arguments, and reference() takes and returns one part's arrays. A program takes and returns all parts, laid end to end along the dimension named above; an argument that names none is the same for every part. Nothing has to cross between parts.
Inputs may be any that keep to these rules, and one draw needn't show every extreme that they name: `block_list`: for each KV head, no logical block appears twice among all rows' lists. `kept_len`: some row of every KV head keeps 16 blocks and some other row keeps one.
All inputs are finite; a program needn't handle non-finite values.
Results may differ from the reference program's by a relative error of at most 0.012.
The reference program's roundings to bfloat16 on the way count: a program that leaves them out, or rounds other values in their place, can miss the bound.
Values may be sent and summed in bfloat16 or wider, within the bound.
No kernel may reach another device: no remote copies, remote signals or barrier semaphores. Data moves between devices by JAX's collectives and lax.ppermute only.
A program may use at most 64 MiB of HBM per device.

```python
import jax
import jax.numpy as jnp
from jax import lax

D = 8192
QUERY_HEADS = 64
KEY_VALUE_HEADS = 8
HEAD_SIZE = 128
BLOCK_TOKENS = 128
DECODED_ROWS = 8
POOL_BLOCKS = 128
KEPT_BLOCKS_MOST = 16


def draw_activations(key, part):
    key_entries, key_cols, key_rows = jax.random.split(jax.random.fold_in(key, 3), 3)
    entries = jax.random.normal(key_entries, (DECODED_ROWS, D), jnp.float32)
    entries = jnp.clip(entries, -6.0, 6.0)
    column_scale = jnp.exp(jnp.log(10.0) * jax.random.uniform(key_cols, (D,), jnp.float32))
    column_scale = column_scale * (1.0 + 2.0 * jnp.arange(D, dtype=jnp.float32) / D)
    row_scale = jnp.exp(jnp.log(10.0) * jax.random.uniform(key_rows, (DECODED_ROWS, 1), jnp.float32))
    return (entries * column_scale * row_scale / 5.0).astype(jnp.bfloat16)


def draw_key_pool(key, part):
    key_noise = jax.random.fold_in(jax.random.fold_in(key, 5), 0)
    full_shape = (KEY_VALUE_HEADS, POOL_BLOCKS, BLOCK_TOKENS, HEAD_SIZE)
    noise_part = jnp.clip(jax.random.normal(key_noise, full_shape, jnp.float32), -4.0, 4.0)
    return noise_part.astype(jnp.bfloat16)


def draw_block_list(key, part):
    keys_per_head = jax.random.split(jax.random.fold_in(key, 11), KEY_VALUE_HEADS)
    shuffled_slots = jax.vmap(lambda head_key: jax.random.permutation(head_key, POOL_BLOCKS))(keys_per_head)
    selected_index = shuffled_slots[:, :DECODED_ROWS * KEPT_BLOCKS_MOST].reshape(KEY_VALUE_HEADS, DECODED_ROWS, KEPT_BLOCKS_MOST)
    return jnp.transpose(selected_index, (1, 0, 2)).astype(jnp.int32)


def draw_kept_len(key, part):
    key_length_draw, key_upper_bound, key_small_scale = jax.random.split(jax.random.fold_in(key, 23), 3)
    row_lengths = jax.random.randint(key_length_draw, (DECODED_ROWS, KEY_VALUE_HEADS), 1, KEPT_BLOCKS_MOST + 1, jnp.int32)
    longest_length = jax.random.randint(key_upper_bound, (1, KEY_VALUE_HEADS), 0, DECODED_ROWS, jnp.int32)
    shortest_length = (longest_length + jax.random.randint(key_small_scale, (1, KEY_VALUE_HEADS), 1, DECODED_ROWS, jnp.int32)) % DECODED_ROWS
    row_ids = jnp.arange(DECODED_ROWS, dtype=jnp.int32)[:, None]
    row_lengths = jnp.where(row_ids == longest_length, KEPT_BLOCKS_MOST, row_lengths)
    row_lengths = jnp.where(row_ids == shortest_length, 1, row_lengths)
    return row_lengths.astype(jnp.int32)


def levels(key, shape, shards, low, top_value):
    def one(axis_at, shards_of):
        draws = jax.random.uniform(jax.random.fold_in(jax.random.fold_in(key, 6), axis_at), (shards_of,), jnp.float32, low / len(shards), top_value / len(shards))
        return jnp.repeat(jnp.exp(draws), shape[axis_at] // shards_of).reshape((-1,) + (1,) * (len(shape) - axis_at - 1))

    loudness = one(*shards[0])
    for cut in shards[1:]:
        loudness = loudness * one(*cut)
    return loudness


def bell_draw(key, shape, spread, bound, cuts=(), kind=jnp.bfloat16):
    values = jax.random.normal(key, shape, jnp.float32) * spread
    if len(cuts) > 0:
        values = levels(key, shape, cuts, -0.22, 0.18) * values
    return jnp.clip(values, min=-bound, max=bound).astype(kind)


def setup_inputs(seed: int = 0, part: int = 0) -> dict:
    key_list = jax.random.split(jax.random.key(seed), 10)
    part_splits = jax.random.split(jax.random.fold_in(key_list[9], part), 10)
    return {
        "activations": draw_activations(jax.random.fold_in(jax.random.fold_in(key_list[9], part), 71), part),
        "norm_gain": jnp.clip(1.0 + 0.18 * jax.random.normal(key_list[1], (D,), jnp.float32), 0.099609375, 1.8984375).astype(jnp.bfloat16),
        "w_query": bell_draw(key_list[2], (D, QUERY_HEADS * HEAD_SIZE), D ** -0.5, 0.0625, ((0, 4), (1, 4))),
        "w_out": bell_draw(key_list[3], (QUERY_HEADS * HEAD_SIZE, D), (QUERY_HEADS * HEAD_SIZE) ** -0.5, 0.0625, ((0, 4), (1, 4))),
        "key_pool": draw_key_pool(jax.random.fold_in(jax.random.fold_in(key_list[9], part), 71), part),
        "value_block_store": bell_draw(part_splits[5], (KEY_VALUE_HEADS, POOL_BLOCKS, BLOCK_TOKENS, HEAD_SIZE), 8.0, 48.0, ((0, 4), (1, 4))),
        "block_list": draw_block_list(jax.random.fold_in(jax.random.fold_in(key_list[9], part), 71), part),
        "block_slot_table": jax.vmap(lambda own: jax.random.permutation(own, POOL_BLOCKS))(jax.random.split(part_splits[7], KEY_VALUE_HEADS)).reshape((KEY_VALUE_HEADS, POOL_BLOCKS)).astype(jnp.int32),
        "kept_len": draw_kept_len(jax.random.fold_in(jax.random.fold_in(key_list[9], part), 71), part),
    }


epsilon = 1e-05

def reference(activations, norm_gain, w_query, w_out, key_pool, value_block_store, block_list, block_slot_table, kept_len):
    features = activations.astype(jnp.float32)
    mean_square = lax.optimization_barrier(jnp.mean(features * features, axis=1))
    scaled = (features * norm_gain.astype(jnp.float32)).astype(jnp.bfloat16)
    projected = jnp.dot(scaled, w_query, preferred_element_type=jnp.float32)
    query_vectors = (projected * lax.rsqrt(mean_square + epsilon)[:, None] * HEAD_SIZE ** (-0.5)).astype(jnp.bfloat16)
    query_vectors = query_vectors.reshape(DECODED_ROWS, KEY_VALUE_HEADS, QUERY_HEADS // KEY_VALUE_HEADS, HEAD_SIZE)
    slot_lookup_table = jnp.broadcast_to(block_slot_table[None], (DECODED_ROWS, KEY_VALUE_HEADS, POOL_BLOCKS))
    slot_ids = jnp.take_along_axis(slot_lookup_table, block_list, axis=2)
    is_live = jnp.arange(KEPT_BLOCKS_MOST, dtype=jnp.int32)[None, None, :] < kept_len[:, :, None]
    kv_head_position = jnp.arange(KEY_VALUE_HEADS, dtype=jnp.int32)[:, None]

    def one_row(packed):
        row_query, row_slots, row_live = packed
        row_keys = key_pool[kv_head_position, row_slots].astype(jnp.float32)
        row_values = value_block_store[kv_head_position, row_slots].astype(jnp.float32)
        scores = jnp.einsum('hgd,hktd->hgkt', row_query.astype(jnp.float32), row_keys)
        scores = jnp.where(row_live[:, None, :, None], scores, -jnp.inf)
        best_score = lax.optimization_barrier(jnp.max(scores, axis=(2, 3), keepdims=True))
        weights_full = jnp.exp(scores - best_score)
        sum_weight = lax.optimization_barrier(jnp.sum(weights_full, axis=(2, 3)))
        rounded = lax.optimization_barrier(weights_full.astype(jnp.bfloat16)).astype(jnp.float32)
        sum_value = jnp.einsum('hgkt,hktd->hgd', rounded, row_values)
        return (sum_value / sum_weight[..., None]).astype(jnp.bfloat16)
    attended = lax.map(one_row, (query_vectors, slot_ids, is_live))
    attended = attended.reshape(DECODED_ROWS, QUERY_HEADS * HEAD_SIZE)
    return jnp.dot(attended, w_out, preferred_element_type=jnp.float32).astype(jnp.bfloat16)
```

```python
import functools

import jax
import jax.numpy as jnp
from jax import lax
from jax.experimental import pallas as pl
from jax.experimental.pallas import tpu as pltpu
from jax.sharding import PartitionSpec as P

very_low = -1e30
epsilon = 1e-05
LANES = 128
DIRECT_MOST = 8
VMEM = pl.BlockSpec(memory_space=pltpu.VMEM)
HBM = pl.BlockSpec(memory_space=pltpu.HBM)


def project_kernel(
    act_ref, gain_ref, list_ref, table_ref, len_ref, w_ref, out_ref, bias_ref, held, sem, *, chunks
):
    depth, columns = w_ref.shape
    step = depth // chunks
    copies = [
        pltpu.make_async_copy(
            w_ref.at[pl.ds(i * step, step)], held.at[pl.ds(i * step, step)], sem.at[i]
        )
        for i in range(chunks)
    ]
    for copy in copies:
        copy.start()
    rows = act_ref.shape[0]
    features = act_ref[...].astype(jnp.float32)
    squares = jnp.sum(features * features, axis=1, keepdims=True)
    out_ref[:, columns:] = jnp.broadcast_to(squares, (rows, LANES))
    scaled = (features * gain_ref[...].astype(jnp.float32)).astype(jnp.bfloat16)

    kv_heads, blocks = table_ref.shape
    kept_most = list_ref.shape[2]
    slots = bias_ref.shape[1]
    first_slot = lax.axis_index("lender") * slots
    logical = lax.broadcasted_iota(jnp.int32, (rows, blocks), 1)
    own_slot = lax.broadcasted_iota(jnp.int32, (slots, blocks), 0) + first_slot
    for h in range(kv_heads):
        listed = list_ref[:, h, :]
        lens = len_ref[:, h : h + 1]
        kept = jnp.zeros((rows, blocks), jnp.float32)
        for k in range(kept_most):
            entry = jnp.where(lens > k, listed[:, k : k + 1], -1)
            kept = jnp.where(entry == logical, 1.0, kept)
        placed = (own_slot == table_ref[h : h + 1, :]).astype(jnp.bfloat16)
        owned = lax.dot_general(
            kept.astype(jnp.bfloat16),
            placed,
            (((1,), (1,)), ((), ())),
            preferred_element_type=jnp.float32,
        )
        bias = jnp.where(owned > 0.5, 0.0, very_low)
        for s in range(slots):
            bias_ref[h, s] = jnp.broadcast_to(bias[:, s : s + 1], (rows, LANES))

    total = jnp.zeros((rows, columns), jnp.float32)
    for i in range(chunks):
        copies[i].wait()
        total = total + jnp.dot(
            scaled[:, i * step : (i + 1) * step],
            held[i * step : (i + 1) * step, :],
            preferred_element_type=jnp.float32,
        )
    out_ref[:, :columns] = total


def tree_sum(parts):
    while len(parts) > 1:
        parts = [a + b for a, b in zip(parts[::2], parts[1::2])] + parts[len(parts) & ~1 :]
    return parts[0]


def attend_kernel(*refs, parts, width):
    part_refs = refs[:parts]
    bias_ref, key_ref, value_ref, out_ref, score_ref, weight_ref = refs[parts:]
    rows = out_ref.shape[0]
    kv_heads, slots, tokens, head_dim = key_ref.shape
    columns = part_refs[0].shape[1] - LANES
    group = columns // (kv_heads * head_dim)
    heads = kv_heads * group
    square_sum = tree_sum([ref[:, columns:] for ref in part_refs])
    inverse = lax.rsqrt(square_sum / width + epsilon)
    lane = lax.broadcasted_iota(jnp.int32, (rows, LANES), 1)
    all_best = jnp.full((rows, LANES), very_low, jnp.float32)
    all_total = jnp.zeros((rows, LANES), jnp.float32)
    for h in range(kv_heads):
        pieces = []
        for g in range(group):
            at = (h * group + g) * head_dim
            projected = tree_sum([ref[:, at : at + head_dim] for ref in part_refs])
            pieces.append(projected * inverse * head_dim ** (-0.5))
        query = jnp.concatenate(pieces, axis=0).astype(jnp.bfloat16)
        best = jnp.full((group, rows, tokens), very_low, jnp.float32)
        for s in range(slots):
            score = lax.dot_general(
                query,
                key_ref[h, s],
                (((1,), (1,)), ((), ())),
                preferred_element_type=jnp.float32,
            ).reshape(group, rows, tokens)
            score = score + bias_ref[h, s][None]
            best = jnp.maximum(best, score)
            score_ref[:, s * tokens : (s + 1) * tokens] = score.reshape(group * rows, tokens)
        best = jnp.max(best.reshape(group * rows, tokens), axis=1, keepdims=True)
        total = jnp.zeros((group * rows, tokens), jnp.float32)
        for s in range(slots):
            weight = jnp.exp(score_ref[:, s * tokens : (s + 1) * tokens] - best)
            total = total + weight
            weight_ref[:, s * tokens : (s + 1) * tokens] = weight.astype(jnp.bfloat16)
        total = jnp.sum(total, axis=1, keepdims=True)
        summed = jnp.dot(
            weight_ref[...],
            value_ref[h].reshape(slots * tokens, head_dim),
            preferred_element_type=jnp.float32,
        )
        for g in range(group):
            j = h * group + g
            out_ref[:, j * head_dim : (j + 1) * head_dim] = summed[g * rows : (g + 1) * rows]
            all_best = jnp.where(lane == j, best[g * rows : (g + 1) * rows], all_best)
            all_total = jnp.where(lane == j, total[g * rows : (g + 1) * rows], all_total)
    out_ref[:, columns : columns + LANES] = all_best
    out_ref[:, columns + LANES :] = all_total


def output_kernel(*refs, parts, peers, head_dim):
    part_refs = refs[:parts]
    w_ref = refs[parts]
    out_refs = refs[parts + 1 :]
    rows = part_refs[0].shape[0]
    columns = w_ref.shape[0]
    bests = [ref[:, columns : columns + LANES] for ref in part_refs]
    highest = functools.reduce(jnp.maximum, bests)
    factors = [jnp.exp(best - highest) for best in bests]
    total = tree_sum(
        [f * ref[:, columns + LANES :] for f, ref in zip(factors, part_refs)]
    )
    shares = [f / total for f in factors]
    pieces = []
    for j in range(columns // head_dim):
        at = j * head_dim
        pieces.append(
            tree_sum(
                [
                    share[:, j : j + 1] * ref[:, at : at + head_dim]
                    for share, ref in zip(shares, part_refs)
                ]
            )
        )
    attended = jnp.concatenate(pieces, axis=1)
    home = rows // peers
    shift = lax.rem((peers - lax.axis_index("tensor")) * home, rows)
    attended = pltpu.roll(attended, shift, 0).astype(jnp.bfloat16)
    result = jnp.dot(attended, w_ref[...], preferred_element_type=jnp.float32)
    for i, ref in enumerate(out_refs):
        ref[...] = result[i * home : (i + 1) * home]


def send_all(value, axis):
    size = lax.axis_size(axis)
    if size > DIRECT_MOST:
        gathered = lax.all_gather(value, axis)
        return [gathered[i] for i in range(size)]
    if size & (size - 1) == 0:
        tables = [[(i, i ^ s) for i in range(size)] for s in range(1, size)]
    else:
        tables = [[(i, (i + s) % size) for i in range(size)] for s in range(1, size)]
    return [value] + [lax.ppermute(value, axis, table) for table in tables]


def per_device(
    activations,
    norm_gain,
    w_query,
    w_out,
    key_pool,
    value_block_store,
    block_list,
    block_slot_table,
    kept_len,
):
    rows = activations.shape[0]
    depth, columns = w_query.shape
    kv_heads, slots, tokens, head_dim = key_pool.shape
    group = columns // (kv_heads * head_dim)
    lenders = lax.axis_size("lender")
    peers = lax.axis_size("tensor")
    chunks = max(1, min(8, depth // 256))

    payload, bias = pl.pallas_call(
        functools.partial(project_kernel, chunks=chunks),
        out_shape=(
            jax.ShapeDtypeStruct((rows, columns + LANES), jnp.float32),
            jax.ShapeDtypeStruct((kv_heads, slots, rows, LANES), jnp.float32),
        ),
        in_specs=[VMEM] * 5 + [HBM],
        out_specs=(VMEM, VMEM),
        scratch_shapes=[
            pltpu.VMEM((depth, columns), jnp.bfloat16),
            pltpu.SemaphoreType.DMA((chunks,)),
        ],
        compiler_params=pltpu.CompilerParams(vmem_limit_bytes=20 << 20),
        name="project",
    )(
        activations,
        norm_gain[None],
        block_list,
        block_slot_table,
        kept_len,
        pltpu.with_memory_space_constraint(w_query, pltpu.HBM),
    )

    if lenders > DIRECT_MOST:
        parts = [lax.psum(payload, "lender")]
    else:
        parts = send_all(payload, "lender")

    partial_state = pl.pallas_call(
        functools.partial(attend_kernel, parts=len(parts), width=depth * lenders),
        out_shape=jax.ShapeDtypeStruct((rows, columns + 2 * LANES), jnp.float32),
        in_specs=[VMEM] * (len(parts) + 3),
        out_specs=VMEM,
        scratch_shapes=[
            pltpu.VMEM((group * rows, slots * tokens), jnp.float32),
            pltpu.VMEM((group * rows, slots * tokens), jnp.bfloat16),
        ],
        compiler_params=pltpu.CompilerParams(vmem_limit_bytes=24 << 20),
        name="attend",
    )(*parts, bias, key_pool, value_block_store)

    parts = send_all(partial_state, "lender")

    home = rows // peers
    sums = pl.pallas_call(
        functools.partial(output_kernel, parts=len(parts), peers=peers, head_dim=head_dim),
        out_shape=[jax.ShapeDtypeStruct((home, w_out.shape[1]), jnp.float32)] * peers,
        in_specs=[VMEM] * (len(parts) + 1),
        out_specs=[VMEM] * peers,
        compiler_params=pltpu.CompilerParams(vmem_limit_bytes=24 << 20),
        name="output",
    )(*parts, w_out)

    result = sums[0]
    for s in range(1, peers):
        result = result + lax.ppermute(
            sums[s], "tensor", [(i, (i + s) % peers) for i in range(peers)]
        )
    return result.astype(jnp.bfloat16)


def solution(mesh):
    in_specs = (
        P("group", "lender"),
        P("lender"),
        P("lender", "tensor"),
        P("tensor", "lender"),
        P("tensor", ("group", "lender"), None, None),
        P("tensor", ("group", "lender"), None, None),
        P("group", "tensor", None),
        P("tensor", "group"),
        P("group", "tensor"),
    )
    out_specs = P(("group", "tensor"), "lender")
    return jax.shard_map(
        per_device, mesh=mesh, in_specs=in_specs, out_specs=out_specs, check_vma=False
    )
```

```python
import functools

import jax
import jax.numpy as jnp
from jax import lax
from jax.experimental import pallas as pl
from jax.experimental.pallas import tpu as pltpu
from jax.sharding import PartitionSpec as P

very_low = -1e30
epsilon = 1e-05
LANES = 128
DIRECT_MOST = 8
VMEM = pl.BlockSpec(memory_space=pltpu.VMEM)
HBM = pl.BlockSpec(memory_space=pltpu.HBM)


def project_kernel(
    act_hbm, gain_hbm, list_hbm, table_hbm, len_hbm, w_hbm, out_ref, bias_ref,
    act_ref, gain_ref, list_ref, table_ref, len_ref, held, small_sem, sem, *, chunks
):
    depth, columns = w_hbm.shape
    step = depth // chunks
    small = [
        pltpu.make_async_copy(source, target, small_sem.at[i])
        for i, (source, target) in enumerate(
            (
                (act_hbm, act_ref),
                (gain_hbm, gain_ref),
                (list_hbm, list_ref),
                (table_hbm, table_ref),
                (len_hbm, len_ref),
            )
        )
    ]
    copies = [
        pltpu.make_async_copy(
            w_hbm.at[pl.ds(i * step, step)], held.at[pl.ds(i * step, step)], sem.at[i]
        )
        for i in range(chunks)
    ]
    for copy in small + copies:
        copy.start()
    for copy in small:
        copy.wait()
    rows = act_ref.shape[0]
    features = act_ref[...].astype(jnp.float32)
    squares = jnp.sum(features * features, axis=1, keepdims=True)
    out_ref[:, columns:] = jnp.broadcast_to(squares, (rows, LANES))
    gain = gain_ref[...].astype(jnp.float32)
    gain = jnp.concatenate(
        [jnp.broadcast_to(gain[i : i + 1], (rows, LANES)) for i in range(depth // LANES)], axis=1
    )
    scaled = (features * gain).astype(jnp.bfloat16)

    kv_heads, blocks = table_ref.shape
    kept_most = list_ref.shape[2]
    slots = bias_ref.shape[1]
    first_slot = lax.axis_index("lender") * slots
    logical = lax.broadcasted_iota(jnp.int32, (rows, blocks), 1)
    own_slot = lax.broadcasted_iota(jnp.int32, (slots, blocks), 0) + first_slot
    diagonal = lax.broadcasted_iota(jnp.int32, (rows, rows), 0) == lax.broadcasted_iota(
        jnp.int32, (rows, rows), 1
    )
    for h in range(kv_heads):
        listed = list_ref[:, h, :]
        lens = jnp.sum(jnp.where(diagonal, len_ref[h : h + 1, :], 0), axis=1, keepdims=True)
        kept = jnp.zeros((rows, blocks), jnp.float32)
        for k in range(kept_most):
            entry = jnp.where(lens > k, listed[:, k : k + 1], -1)
            kept = jnp.where(entry == logical, 1.0, kept)
        placed = (own_slot == table_ref[h : h + 1, :]).astype(jnp.bfloat16)
        owned = lax.dot_general(
            kept.astype(jnp.bfloat16),
            placed,
            (((1,), (1,)), ((), ())),
            preferred_element_type=jnp.float32,
        )
        bias = jnp.where(owned > 0.5, 0.0, very_low)
        for s in range(slots):
            bias_ref[h, s] = jnp.broadcast_to(bias[:, s : s + 1], (rows, LANES))

    total = jnp.zeros((rows, columns), jnp.float32)
    for i in range(chunks):
        copies[i].wait()
        total = total + jnp.dot(
            scaled[:, i * step : (i + 1) * step],
            held[i * step : (i + 1) * step, :],
            preferred_element_type=jnp.float32,
        )
    out_ref[:, :columns] = total


def tree_sum(parts):
    while len(parts) > 1:
        parts = [a + b for a, b in zip(parts[::2], parts[1::2])] + parts[len(parts) & ~1 :]
    return parts[0]


def attend_kernel(*refs, parts, width):
    part_refs = refs[:parts]
    bias_ref, key_ref, value_ref, out_ref, score_ref, weight_ref = refs[parts:]
    rows = out_ref.shape[0]
    kv_heads, slots, tokens, head_dim = key_ref.shape
    columns = part_refs[0].shape[1] - LANES
    group = columns // (kv_heads * head_dim)
    heads = kv_heads * group
    square_sum = tree_sum([ref[:, columns:] for ref in part_refs])
    inverse = lax.rsqrt(square_sum / width + epsilon)
    lane = lax.broadcasted_iota(jnp.int32, (rows, LANES), 1)
    all_best = jnp.full((rows, LANES), very_low, jnp.float32)
    all_total = jnp.zeros((rows, LANES), jnp.float32)
    for h in range(kv_heads):
        pieces = []
        for g in range(group):
            at = (h * group + g) * head_dim
            projected = tree_sum([ref[:, at : at + head_dim] for ref in part_refs])
            pieces.append(projected * inverse * head_dim ** (-0.5))
        query = jnp.concatenate(pieces, axis=0).astype(jnp.bfloat16)
        best = jnp.full((group, rows, tokens), very_low, jnp.float32)
        for s in range(slots):
            score = lax.dot_general(
                query,
                key_ref[h, s],
                (((1,), (1,)), ((), ())),
                preferred_element_type=jnp.float32,
            ).reshape(group, rows, tokens)
            score = score + bias_ref[h, s][None]
            best = jnp.maximum(best, score)
            score_ref[:, s * tokens : (s + 1) * tokens] = score.reshape(group * rows, tokens)
        best = jnp.max(best.reshape(group * rows, tokens), axis=1, keepdims=True)
        total = jnp.zeros((group * rows, tokens), jnp.float32)
        for s in range(slots):
            weight = jnp.exp(score_ref[:, s * tokens : (s + 1) * tokens] - best)
            total = total + weight
            weight_ref[:, s * tokens : (s + 1) * tokens] = weight.astype(jnp.bfloat16)
        total = jnp.sum(total, axis=1, keepdims=True)
        summed = jnp.dot(
            weight_ref[...],
            value_ref[h].reshape(slots * tokens, head_dim),
            preferred_element_type=jnp.float32,
        )
        for g in range(group):
            j = h * group + g
            out_ref[:, j * head_dim : (j + 1) * head_dim] = summed[g * rows : (g + 1) * rows]
            all_best = jnp.where(lane == j, best[g * rows : (g + 1) * rows], all_best)
            all_total = jnp.where(lane == j, total[g * rows : (g + 1) * rows], all_total)
    out_ref[:, columns : columns + LANES] = all_best
    out_ref[:, columns + LANES :] = all_total


def output_kernel(*refs, parts, peers, head_dim):
    part_refs = refs[:parts]
    w_ref = refs[parts]
    out_refs = refs[parts + 1 :]
    rows = part_refs[0].shape[0]
    columns = w_ref.shape[0]
    bests = [ref[:, columns : columns + LANES] for ref in part_refs]
    highest = functools.reduce(jnp.maximum, bests)
    factors = [jnp.exp(best - highest) for best in bests]
    total = tree_sum(
        [f * ref[:, columns + LANES :] for f, ref in zip(factors, part_refs)]
    )
    shares = [f / total for f in factors]
    pieces = []
    for j in range(columns // head_dim):
        at = j * head_dim
        pieces.append(
            tree_sum(
                [
                    share[:, j : j + 1] * ref[:, at : at + head_dim]
                    for share, ref in zip(shares, part_refs)
                ]
            )
        )
    attended = jnp.concatenate(pieces, axis=1)
    home = rows // peers
    shift = lax.rem((peers - lax.axis_index("tensor")) * home, rows)
    attended = pltpu.roll(attended, shift, 0).astype(jnp.bfloat16)
    result = jnp.dot(attended, w_ref[...], preferred_element_type=jnp.float32)
    for i, ref in enumerate(out_refs):
        ref[...] = result[i * home : (i + 1) * home]


def send_all(value, axis):
    size = lax.axis_size(axis)
    if size > DIRECT_MOST:
        gathered = lax.all_gather(value, axis)
        return [gathered[i] for i in range(size)]
    if size & (size - 1) == 0:
        tables = [[(i, i ^ s) for i in range(size)] for s in range(1, size)]
    else:
        tables = [[(i, (i + s) % size) for i in range(size)] for s in range(1, size)]
    return [value] + [lax.ppermute(value, axis, table) for table in tables]


def per_device(
    activations,
    norm_gain,
    w_query,
    w_out,
    key_pool,
    value_block_store,
    block_list,
    block_slot_table,
    kept_len,
):
    rows = activations.shape[0]
    depth, columns = w_query.shape
    kv_heads, slots, tokens, head_dim = key_pool.shape
    group = columns // (kv_heads * head_dim)
    lenders = lax.axis_size("lender")
    peers = lax.axis_size("tensor")
    chunks = max(1, min(8, depth // 256))

    payload, bias = pl.pallas_call(
        functools.partial(project_kernel, chunks=chunks),
        out_shape=(
            jax.ShapeDtypeStruct((rows, columns + LANES), jnp.float32),
            jax.ShapeDtypeStruct((kv_heads, slots, rows, LANES), jnp.float32),
        ),
        in_specs=[HBM] * 6,
        out_specs=(VMEM, VMEM),
        scratch_shapes=[
            pltpu.VMEM(activations.shape, activations.dtype),
            pltpu.VMEM((depth // LANES, LANES), norm_gain.dtype),
            pltpu.VMEM(block_list.shape, block_list.dtype),
            pltpu.VMEM(block_slot_table.shape, block_slot_table.dtype),
            pltpu.VMEM(kept_len.shape[::-1], kept_len.dtype),
            pltpu.VMEM((depth, columns), jnp.bfloat16),
            pltpu.SemaphoreType.DMA((5,)),
            pltpu.SemaphoreType.DMA((chunks,)),
        ],
        compiler_params=pltpu.CompilerParams(vmem_limit_bytes=20 << 20),
        name="project",
    )(
        *(
            pltpu.with_memory_space_constraint(value, pltpu.HBM)
            for value in (
                activations,
                norm_gain.reshape(-1, LANES),
                block_list,
                block_slot_table,
                kept_len.T,
                w_query,
            )
        )
    )
    payload, key_pool, value_block_store, w_out = lax.optimization_barrier(
        (payload, key_pool, value_block_store, w_out)
    )

    if lenders > DIRECT_MOST:
        parts = [lax.psum(payload, "lender")]
    else:
        parts = send_all(payload, "lender")

    partial_state = pl.pallas_call(
        functools.partial(attend_kernel, parts=len(parts), width=depth * lenders),
        out_shape=jax.ShapeDtypeStruct((rows, columns + 2 * LANES), jnp.float32),
        in_specs=[VMEM] * (len(parts) + 3),
        out_specs=VMEM,
        scratch_shapes=[
            pltpu.VMEM((group * rows, slots * tokens), jnp.float32),
            pltpu.VMEM((group * rows, slots * tokens), jnp.bfloat16),
        ],
        compiler_params=pltpu.CompilerParams(vmem_limit_bytes=24 << 20),
        name="attend",
    )(*parts, bias, key_pool, value_block_store)

    parts = send_all(partial_state, "lender")

    home = rows // peers
    sums = pl.pallas_call(
        functools.partial(output_kernel, parts=len(parts), peers=peers, head_dim=head_dim),
        out_shape=[jax.ShapeDtypeStruct((home, w_out.shape[1]), jnp.float32)] * peers,
        in_specs=[VMEM] * (len(parts) + 1),
        out_specs=[VMEM] * peers,
        compiler_params=pltpu.CompilerParams(vmem_limit_bytes=24 << 20),
        name="output",
    )(*parts, w_out)

    result = sums[0]
    for s in range(1, peers):
        result = result + lax.ppermute(
            sums[s], "tensor", [(i, (i + s) % peers) for i in range(peers)]
        )
    return result.astype(jnp.bfloat16)


def solution(mesh):
    in_specs = (
        P("group", "lender"),
        P("lender"),
        P("lender", "tensor"),
        P("tensor", "lender"),
        P("tensor", ("group", "lender"), None, None),
        P("tensor", ("group", "lender"), None, None),
        P("group", "tensor", None),
        P("tensor", "group"),
        P("group", "tensor"),
    )
    out_specs = P(("group", "tensor"), "lender")
    return jax.shard_map(
        per_device, mesh=mesh, in_specs=in_specs, out_specs=out_specs, check_vma=False
    )
```

```python
import functools

import jax
import jax.numpy as jnp
from jax import lax
from jax.experimental import pallas as pl
from jax.experimental.pallas import tpu as pltpu
from jax.sharding import PartitionSpec as P

very_low = -1e30
epsilon = 1e-05
LANES = 128
DIRECT_MOST = 8
VMEM = pl.BlockSpec(memory_space=pltpu.VMEM)
HBM = pl.BlockSpec(memory_space=pltpu.HBM)


def project_kernel(act_hbm, gain_hbm, w_hbm, out_ref, act_ref, gain_ref, held, small_sem, sem):
    depth, columns = w_hbm.shape
    chunks = sem.shape[0]
    step = depth // chunks
    small = [
        pltpu.make_async_copy(act_hbm, act_ref, small_sem.at[0]),
        pltpu.make_async_copy(gain_hbm, gain_ref, small_sem.at[1]),
    ]
    copies = [
        pltpu.make_async_copy(
            w_hbm.at[pl.ds(i * step, step)], held.at[pl.ds(i * step, step)], sem.at[i]
        )
        for i in range(chunks)
    ]
    for copy in small + copies:
        copy.start()
    for copy in small:
        copy.wait()
    rows = act_ref.shape[0]
    features = act_ref[...].astype(jnp.float32)
    squares = jnp.sum(features * features, axis=1, keepdims=True)
    out_ref[:, columns:] = jnp.broadcast_to(squares, (rows, LANES))
    gain = gain_ref[...].astype(jnp.float32)
    gain = jnp.concatenate(
        [jnp.broadcast_to(gain[i : i + 1], (rows, LANES)) for i in range(depth // LANES)], axis=1
    )
    scaled = (features * gain).astype(jnp.bfloat16)
    total = jnp.zeros((rows, columns), jnp.float32)
    for i in range(chunks):
        copies[i].wait()
        total = total + jnp.dot(
            scaled[:, i * step : (i + 1) * step],
            held[i * step : (i + 1) * step, :],
            preferred_element_type=jnp.float32,
        )
    out_ref[:, :columns] = total


def pools_kernel(
    after_hbm, list_hbm, table_hbm, len_hbm, key_hbm, value_hbm, key_ref, value_ref, bias_ref,
    list_ref, table_ref, len_ref, sem
):
    pairs = (
        (list_hbm, list_ref),
        (table_hbm, table_ref),
        (len_hbm, len_ref),
        (key_hbm, key_ref),
        (value_hbm, value_ref),
    )
    copies = [pltpu.make_async_copy(*pair, sem.at[i]) for i, pair in enumerate(pairs)]
    for copy in copies:
        copy.start()
    for copy in copies[:3]:
        copy.wait()
    kv_heads, slots, rows, _ = bias_ref.shape
    blocks = table_ref.shape[1]
    kept_most = list_ref.shape[2]
    first_slot = lax.axis_index("lender") * slots
    logical = lax.broadcasted_iota(jnp.int32, (rows, blocks), 1)
    own_slot = lax.broadcasted_iota(jnp.int32, (slots, blocks), 0) + first_slot
    diagonal = lax.broadcasted_iota(jnp.int32, (rows, rows), 0) == lax.broadcasted_iota(
        jnp.int32, (rows, rows), 1
    )
    for h in range(kv_heads):
        listed = list_ref[:, h, :]
        lens = jnp.sum(jnp.where(diagonal, len_ref[h : h + 1, :], 0), axis=1, keepdims=True)
        kept = jnp.zeros((rows, blocks), jnp.float32)
        for k in range(kept_most):
            entry = jnp.where(lens > k, listed[:, k : k + 1], -1)
            kept = jnp.where(entry == logical, 1.0, kept)
        placed = (own_slot == table_ref[h : h + 1, :]).astype(jnp.bfloat16)
        owned = lax.dot_general(
            kept.astype(jnp.bfloat16),
            placed,
            (((1,), (1,)), ((), ())),
            preferred_element_type=jnp.float32,
        )
        bias = jnp.where(owned > 0.5, 0.0, very_low)
        for s in range(slots):
            bias_ref[h, s] = jnp.broadcast_to(bias[:, s : s + 1], (rows, LANES))
    for copy in copies[3:]:
        copy.wait()


def in_three(value):
    pieces = []
    for _ in range(3):
        piece = value.astype(jnp.bfloat16)
        pieces.append(piece)
        value = value - piece.astype(jnp.float32)
    return pieces


def state_blocks(heads):
    per_tile = max(1, min(6, LANES // heads))
    return [((k % per_tile) * heads, k // per_tile) for k in range(6)], -(-6 // per_tile)


def tree_sum(parts):
    while len(parts) > 1:
        parts = [a + b for a, b in zip(parts[::2], parts[1::2])] + parts[len(parts) & ~1 :]
    return parts[0]


def load_kernel(*refs, count):
    sources, targets, sem = refs[1 : 1 + count], refs[1 + count : 1 + 2 * count], refs[-1]
    copies = [
        pltpu.make_async_copy(source, target, sem.at[i])
        for i, (source, target) in enumerate(zip(sources, targets))
    ]
    for copy in copies:
        copy.start()
    for copy in copies:
        copy.wait()


def in_hbm(*arrays):
    return [pltpu.with_memory_space_constraint(a, pltpu.HBM) for a in arrays]


def load(name, after, *arrays):
    count = len(arrays)
    size = sum(a.size * a.dtype.itemsize for a in arrays)
    return pl.pallas_call(
        functools.partial(load_kernel, count=count),
        out_shape=[jax.ShapeDtypeStruct(a.shape, a.dtype) for a in arrays],
        in_specs=[pl.BlockSpec(memory_space=pl.ANY)] + [HBM] * count,
        out_specs=[VMEM] * count,
        scratch_shapes=[pltpu.SemaphoreType.DMA((count,))],
        compiler_params=pltpu.CompilerParams(vmem_limit_bytes=4 << 20),
        cost_estimate=pl.CostEstimate(flops=0, bytes_accessed=size, transcendentals=0),
        name=name,
    )(after, *in_hbm(*arrays))


def attend_kernel(*refs, parts, width):
    part_refs = refs[:parts]
    bias_ref, key_ref, value_ref, out_ref, score_ref, weight_ref = refs[parts:]
    rows = out_ref.shape[0]
    kv_heads, slots, tokens, head_dim = key_ref.shape
    columns = part_refs[0].shape[1] - LANES
    group = columns // (kv_heads * head_dim)
    heads = kv_heads * group
    both = 2 if kv_heads % 2 == 0 else 1
    lines = group * rows
    some = 2 if slots % 2 == 0 else 1
    square_sum = tree_sum([ref[:, columns:] for ref in part_refs])
    inverse = lax.rsqrt(square_sum / width + epsilon)
    lane = lax.broadcasted_iota(jnp.int32, (rows, LANES), 1)
    places, tiles = state_blocks(heads)
    state = [jnp.zeros((rows, LANES), jnp.float32) for _ in range(tiles)]
    for first in range(0, kv_heads, both):
        pieces = []
        for i in range(both):
            blocks = []
            for g in range(group):
                at = ((first + i) * group + g) * head_dim
                projected = tree_sum([ref[:, at : at + head_dim] for ref in part_refs])
                blocks.append(projected * inverse * head_dim ** (-0.5))
            query = jnp.concatenate(blocks, axis=0).astype(jnp.bfloat16)
            row = [jnp.zeros_like(query)] * both
            row[i] = query
            pieces.append(jnp.concatenate(row, axis=1))
        query = jnp.concatenate(pieces, axis=0)
        best = jnp.full((both, group, rows, tokens), very_low, jnp.float32)
        for s in range(0, slots, some):
            keys = jnp.concatenate(
                [
                    key_ref[first + i, s : s + some].reshape(some * tokens, head_dim)
                    for i in range(both)
                ],
                axis=1,
            )
            score = lax.dot_general(
                query, keys, (((1,), (1,)), ((), ())), preferred_element_type=jnp.float32
            )
            for n in range(some):
                piece = score[:, n * tokens : (n + 1) * tokens]
                piece = piece.reshape(both, group, rows, tokens)
                piece = piece + bias_ref[first : first + both, s + n][:, None]
                best = jnp.maximum(best, piece)
                score_ref[:, (s + n) * tokens : (s + n + 1) * tokens] = piece.reshape(
                    both * lines, tokens
                )
        best = jnp.max(best.reshape(both * lines, tokens), axis=1, keepdims=True)
        total = jnp.zeros((both * lines, tokens), jnp.float32)
        for s in range(slots):
            weight = jnp.exp(score_ref[:, s * tokens : (s + 1) * tokens] - best)
            total = total + weight
            weight_ref[:, s * tokens : (s + 1) * tokens] = weight.astype(jnp.bfloat16)
        total = jnp.sum(total, axis=1, keepdims=True)
        summed = jnp.zeros((both * lines, both * head_dim), jnp.float32)
        for s in range(0, slots, some):
            values = jnp.concatenate(
                [
                    value_ref[first + i, s : s + some].reshape(some * tokens, head_dim)
                    for i in range(both)
                ],
                axis=1,
            )
            summed = summed + jnp.dot(
                weight_ref[:, s * tokens : (s + some) * tokens],
                values,
                preferred_element_type=jnp.float32,
            )
        for i in range(both):
            for g in range(group):
                j = (first + i) * group + g
                at = i * lines + g * rows
                out_ref[:, j * head_dim : (j + 1) * head_dim] = summed[
                    at : at + rows, i * head_dim : (i + 1) * head_dim
                ].astype(out_ref.dtype)
                pieces = in_three(best[at : at + rows]) + in_three(total[at : at + rows])
                for piece, (offset, tile) in zip(pieces, places):
                    state[tile] = jnp.where(
                        lane == offset + j, piece.astype(jnp.float32), state[tile]
                    )
    for tile in range(tiles):
        at = columns + tile * LANES
        out_ref[:, at : at + LANES] = state[tile].astype(out_ref.dtype)


def output_kernel(*refs, parts, peers, head_dim):
    part_refs = refs[:parts]
    w_ref = refs[parts]
    out_refs = refs[parts + 1 :]
    rows = part_refs[0].shape[0]
    columns = w_ref.shape[0]
    heads = columns // head_dim
    places, _ = state_blocks(heads)
    bests, totals = [], []
    for ref in part_refs:
        pieces = []
        for offset, tile in places:
            at = columns + tile * LANES
            block = ref[:, at : at + LANES].astype(jnp.float32)
            pieces.append(pltpu.roll(block, (LANES - offset) % LANES, 1))
        bests.append(pieces[0] + pieces[1] + pieces[2])
        totals.append(pieces[3] + pieces[4] + pieces[5])
    highest = functools.reduce(jnp.maximum, bests)
    factors = [jnp.exp(best - highest) for best in bests]
    total = tree_sum([f * t for f, t in zip(factors, totals)])
    shares = [f / total for f in factors]
    pieces = []
    for j in range(heads):
        at = j * head_dim
        pieces.append(
            tree_sum(
                [
                    share[:, j : j + 1] * ref[:, at : at + head_dim].astype(jnp.float32)
                    for share, ref in zip(shares, part_refs)
                ]
            )
        )
    attended = jnp.concatenate(pieces, axis=1)
    home = rows // peers
    shift = lax.rem((peers - lax.axis_index("tensor")) * home, rows)
    attended = pltpu.roll(attended, shift, 0).astype(jnp.bfloat16)
    result = jnp.dot(attended, w_ref[...], preferred_element_type=jnp.float32)
    for i, ref in enumerate(out_refs):
        ref[...] = result[i * home : (i + 1) * home]


def send_all(value, axis):
    size = lax.axis_size(axis)
    if size > DIRECT_MOST:
        gathered = lax.all_gather(value, axis)
        return [gathered[i] for i in range(size)]
    if size & (size - 1) == 0:
        tables = [[(i, i ^ s) for i in range(size)] for s in range(1, size)]
    else:
        tables = [[(i, (i + s) % size) for i in range(size)] for s in range(1, size)]
    return [value] + [lax.ppermute(value, axis, table) for table in tables]


def per_device(
    activations,
    norm_gain,
    w_query,
    w_out,
    key_pool,
    value_block_store,
    block_list,
    block_slot_table,
    kept_len,
):
    rows = activations.shape[0]
    depth, columns = w_query.shape
    kv_heads, slots, tokens, head_dim = key_pool.shape
    group = columns // (kv_heads * head_dim)
    lenders = lax.axis_size("lender")
    peers = lax.axis_size("tensor")
    both = 2 if kv_heads % 2 == 0 else 1
    chunks = max(1, min(4, depth // 256))

    payload = pl.pallas_call(
        project_kernel,
        out_shape=jax.ShapeDtypeStruct((rows, columns + LANES), jnp.float32),
        in_specs=[HBM] * 3,
        out_specs=VMEM,
        scratch_shapes=[
            pltpu.VMEM(activations.shape, activations.dtype),
            pltpu.VMEM((depth // LANES, LANES), norm_gain.dtype),
            pltpu.VMEM((depth, columns), jnp.bfloat16),
            pltpu.SemaphoreType.DMA((2,)),
            pltpu.SemaphoreType.DMA((chunks,)),
        ],
        compiler_params=pltpu.CompilerParams(vmem_limit_bytes=12 << 20),
        name="project",
    )(*in_hbm(activations, norm_gain.reshape(-1, LANES), w_query))

    key_pool, value_block_store, bias = pl.pallas_call(
        pools_kernel,
        out_shape=(
            jax.ShapeDtypeStruct(key_pool.shape, key_pool.dtype),
            jax.ShapeDtypeStruct(value_block_store.shape, value_block_store.dtype),
            jax.ShapeDtypeStruct((kv_heads, slots, rows, LANES), jnp.float32),
        ),
        in_specs=[pl.BlockSpec(memory_space=pl.ANY)] + [HBM] * 5,
        out_specs=[VMEM] * 3,
        scratch_shapes=[
            pltpu.VMEM(block_list.shape, block_list.dtype),
            pltpu.VMEM(block_slot_table.shape, block_slot_table.dtype),
            pltpu.VMEM(kept_len.shape[::-1], kept_len.dtype),
            pltpu.SemaphoreType.DMA((5,)),
        ],
        compiler_params=pltpu.CompilerParams(vmem_limit_bytes=12 << 20),
        cost_estimate=pl.CostEstimate(
            flops=0, bytes_accessed=4 * key_pool.size, transcendentals=0
        ),
        name="pools",
    )(
        payload,
        *in_hbm(block_list, block_slot_table, kept_len.T, key_pool, value_block_store),
    )

    if lenders > DIRECT_MOST:
        parts = [lax.psum(payload, "lender")]
    else:
        parts = send_all(payload, "lender")

    tiles = state_blocks(kv_heads * group)[1]
    partial_state = pl.pallas_call(
        functools.partial(attend_kernel, parts=len(parts), width=depth * lenders),
        out_shape=jax.ShapeDtypeStruct((rows, columns + tiles * LANES), jnp.bfloat16),
        in_specs=[VMEM] * (len(parts) + 3),
        out_specs=VMEM,
        scratch_shapes=[
            pltpu.VMEM((both * group * rows, slots * tokens), jnp.float32),
            pltpu.VMEM((both * group * rows, slots * tokens), jnp.bfloat16),
        ],
        compiler_params=pltpu.CompilerParams(vmem_limit_bytes=24 << 20),
        name="attend",
    )(*parts, bias, key_pool, value_block_store)

    parts = send_all(partial_state, "lender")
    (w_out,) = load("load_w_out", partial_state, w_out)

    home = rows // peers
    sums = pl.pallas_call(
        functools.partial(output_kernel, parts=len(parts), peers=peers, head_dim=head_dim),
        out_shape=[jax.ShapeDtypeStruct((home, w_out.shape[1]), jnp.float32)] * peers,
        in_specs=[VMEM] * (len(parts) + 1),
        out_specs=[VMEM] * peers,
        compiler_params=pltpu.CompilerParams(vmem_limit_bytes=24 << 20),
        name="output",
    )(*parts, w_out)

    result = sums[0]
    for s in range(1, peers):
        result = result + lax.ppermute(
            sums[s], "tensor", [(i, (i + s) % peers) for i in range(peers)]
        )
    return result.astype(jnp.bfloat16)


def solution(mesh):
    in_specs = (
        P("group", "lender"),
        P("lender"),
        P("lender", "tensor"),
        P("tensor", "lender"),
        P("tensor", ("group", "lender"), None, None),
        P("tensor", ("group", "lender"), None, None),
        P("group", "tensor", None),
        P("tensor", "group"),
        P("group", "tensor"),
    )
    out_specs = P(("group", "tensor"), "lender")
    return jax.shard_map(
        per_device, mesh=mesh, in_specs=in_specs, out_specs=out_specs, check_vma=False
    )
```

```python
import functools

import jax
import jax.numpy as jnp
from jax import lax
from jax.experimental import pallas as pl
from jax.experimental.pallas import tpu as pltpu
from jax.sharding import PartitionSpec as P

very_low = -1e30
epsilon = 1e-05
LANES = 128
DIRECT_MOST = 8
VMEM = pl.BlockSpec(memory_space=pltpu.VMEM)
HBM = pl.BlockSpec(memory_space=pltpu.HBM)


def in_three(value):
    pieces = []
    for _ in range(3):
        piece = value.astype(jnp.bfloat16)
        pieces.append(piece)
        value = value - piece.astype(jnp.float32)
    return pieces


def project_kernel(
    act_hbm, gain_hbm, w_hbm, out_ref, act_ref, gain_ref, held, small_sem, sem
):
    depth, columns = w_hbm.shape
    chunks = sem.shape[0]
    step = depth // chunks
    small = [
        pltpu.make_async_copy(act_hbm, act_ref, small_sem.at[0]),
        pltpu.make_async_copy(gain_hbm, gain_ref, small_sem.at[1]),
    ]
    copies = [
        pltpu.make_async_copy(
            w_hbm.at[pl.ds(i * step, step)], held.at[pl.ds(i * step, step)], sem.at[i]
        )
        for i in range(chunks)
    ]
    for copy in small + copies:
        copy.start()
    for copy in small:
        copy.wait()
    rows = act_ref.shape[0]
    features = act_ref[...].astype(jnp.float32)
    squares = jnp.sum(features * features, axis=1, keepdims=True)
    out_ref[:, columns:] = jnp.broadcast_to(squares, (rows, LANES))
    gain = gain_ref[...].astype(jnp.float32)
    gain = jnp.concatenate(
        [jnp.broadcast_to(gain[i : i + 1], (rows, LANES)) for i in range(depth // LANES)], axis=1
    )
    scaled = (features * gain).astype(jnp.bfloat16)
    total = jnp.zeros((rows, columns), jnp.float32)
    for i in range(chunks):
        copies[i].wait()
        total = total + jnp.dot(
            scaled[:, i * step : (i + 1) * step],
            held[i * step : (i + 1) * step, :],
            preferred_element_type=jnp.float32,
        )
    out_ref[:, :columns] = total


def owners_kernel(
    after_hbm, list_hbm, table_hbm, len_hbm, pick_ref, gather_ref, bias_ref,
    list_ref, table_ref, len_ref, sem
):
    pairs = ((list_hbm, list_ref), (table_hbm, table_ref), (len_hbm, len_ref))
    copies = [pltpu.make_async_copy(*pair, sem.at[i]) for i, pair in enumerate(pairs)]
    for copy in copies:
        copy.start()
    for copy in copies:
        copy.wait()
    kv_heads, spots, lines = pick_ref.shape
    rows, _, kept_most = list_ref.shape
    blocks = table_ref.shape[1]
    group = lines // rows
    first_slot = lax.axis_index("lender") * (spots // group)
    logical = lax.broadcasted_iota(jnp.int32, (rows, blocks), 1)
    own_slot = lax.broadcasted_iota(jnp.int32, (spots, blocks), 0) // group + first_slot
    diagonal = lax.broadcasted_iota(jnp.int32, (rows, rows), 0) == lax.broadcasted_iota(
        jnp.int32, (rows, rows), 1
    )
    pick_mask = lax.rem(lax.broadcasted_iota(jnp.int32, (spots, lines), 0), group) == (
        lax.broadcasted_iota(jnp.int32, (spots, lines), 1) // rows
    )
    gather_mask = lax.rem(lax.broadcasted_iota(jnp.int32, (lines, spots), 1), group) == (
        lax.broadcasted_iota(jnp.int32, (lines, spots), 0) // rows
    )
    for h in range(kv_heads):
        listed = list_ref[:, h, :]
        lens = jnp.sum(jnp.where(diagonal, len_ref[h : h + 1, :], 0), axis=1, keepdims=True)
        kept = jnp.zeros((rows, blocks), jnp.float32)
        for k in range(kept_most):
            entry = jnp.where(lens > k, listed[:, k : k + 1], -1)
            kept = jnp.where(entry == logical, 1.0, kept)
        kept = jnp.concatenate([kept] * group, axis=0).astype(jnp.bfloat16)
        placed = jnp.where(own_slot == table_ref[h : h + 1, :], 1.0, 0.0).astype(jnp.bfloat16)
        last = (((1,), (1,)), ((), ()))
        owned = lax.dot_general(placed, kept, last, preferred_element_type=jnp.float32)
        owned = jnp.where(pick_mask, owned, 0.0)
        pick_ref[h] = owned.astype(jnp.bfloat16)
        bias_ref[h] = jnp.where(owned > 0.5, 0.0, very_low)
        owned = lax.dot_general(kept, placed, last, preferred_element_type=jnp.float32)
        gather_ref[h] = jnp.where(gather_mask, owned, 0.0).astype(jnp.bfloat16)


def state_blocks(heads):
    per_tile = max(1, min(6, LANES // heads))
    return [((k % per_tile) * heads, k // per_tile) for k in range(6)], -(-6 // per_tile)


def tree_sum(parts):
    while len(parts) > 1:
        parts = [a + b for a, b in zip(parts[::2], parts[1::2])] + parts[len(parts) & ~1 :]
    return parts[0]


def in_hbm(*arrays):
    return [pltpu.with_memory_space_constraint(a, pltpu.HBM) for a in arrays]


def attend_kernel(*refs, parts, width):
    part_refs = refs[:parts]
    pick_ref, gather_ref, bias_ref, key_ref, value_ref, out_ref = refs[parts:]
    rows = out_ref.shape[0]
    kv_heads, slots, tokens, head_dim = key_ref.shape
    columns = part_refs[0].shape[1] - LANES
    group = columns // (kv_heads * head_dim)
    heads = kv_heads * group
    lines = group * rows
    both = 2 if kv_heads % 2 == 0 else 1
    some = 2 if slots % 2 == 0 else 1
    square_sum = tree_sum([ref[:, columns:] for ref in part_refs])
    inverse = lax.rsqrt(square_sum / width + epsilon)
    lane = lax.broadcasted_iota(jnp.int32, (rows, LANES), 1)
    line = lax.broadcasted_iota(jnp.int32, (rows, lines), 1)
    row = lax.broadcasted_iota(jnp.int32, (rows, lines), 0)
    all_best = jnp.zeros((rows, LANES), jnp.float32)
    all_total = jnp.zeros((rows, LANES), jnp.float32)
    for first in range(0, kv_heads, both):
        chosen = []
        for i in range(both):
            blocks = []
            for g in range(group):
                at = ((first + i) * group + g) * head_dim
                projected = tree_sum([ref[:, at : at + head_dim] for ref in part_refs])
                blocks.append(projected * inverse * head_dim ** (-0.5))
            query = jnp.concatenate(blocks, axis=0).astype(jnp.bfloat16)
            chosen.append(
                jnp.dot(pick_ref[first + i], query, preferred_element_type=jnp.float32)
            )
        bests = [[] for _ in range(both)]
        totals = [[] for _ in range(both)]
        values = [[] for _ in range(both)]

        def spread(pieces, at, count):
            zero = jnp.zeros_like(pieces[0])
            lined = [
                jnp.concatenate([p if c == where else zero for c in range(count)], axis=1)
                for p, where in zip(pieces, at)
            ]
            return jnp.concatenate(lined, axis=0).astype(jnp.bfloat16)

        def stacked(ref, s):
            return jnp.concatenate(
                [ref[first + i, s : s + some].reshape(some * tokens, head_dim) for i in range(both)],
                axis=1,
            )

        pairs = [(n, i) for n in range(some) for i in range(both)]
        scores, weights = [], []
        for s in range(0, slots, some):
            query = spread(
                [chosen[i][(s + n) * group : (s + n + 1) * group] for n, i in pairs],
                [i for _, i in pairs],
                both,
            )
            score = lax.dot_general(
                query,
                stacked(key_ref, s),
                (((1,), (1,)), ((), ())),
                preferred_element_type=jnp.float32,
            )
            scores += [
                score[at * group : (at + 1) * group, n * tokens : (n + 1) * tokens]
                for at, (n, i) in enumerate(pairs)
            ]
        for at, score in enumerate(scores):
            best = jnp.max(score, axis=1, keepdims=True)
            weight = jnp.exp(score - best)
            i = pairs[at % len(pairs)][1]
            bests[i].append(best)
            totals[i].append(jnp.sum(weight, axis=1, keepdims=True))
            weights.append(weight)
        for s in range(0, slots, some):
            at = s // some * len(pairs)
            summed = jnp.dot(
                spread(weights[at : at + len(pairs)], [n for n, _ in pairs], some),
                stacked(value_ref, s),
                preferred_element_type=jnp.float32,
            )
            for at, (n, i) in enumerate(pairs):
                values[i].append(
                    summed[at * group : (at + 1) * group, i * head_dim : (i + 1) * head_dim]
                )
        for i in range(both):
            h = first + i
            marked = [
                bias_ref[h, s * group : (s + 1) * group, :] + best
                for s, best in enumerate(bests[i])
            ]
            highest = jnp.max(functools.reduce(jnp.maximum, marked), axis=0, keepdims=True)
            against = jnp.maximum(highest, 0.5 * very_low)
            factors = [jnp.exp(m - against) for m in marked]
            total = jnp.sum(
                tree_sum([f * t for f, t in zip(factors, totals[i])]), axis=0, keepdims=True
            )
            scaled = jnp.concatenate(
                [
                    jnp.sum(f, axis=1, keepdims=True) * v
                    for f, v in zip(factors, values[i])
                ],
                axis=0,
            )
            high = scaled.astype(jnp.bfloat16)
            low = (scaled - high.astype(jnp.float32)).astype(jnp.bfloat16)
            summed = jnp.dot(
                gather_ref[h],
                jnp.concatenate([high, low], axis=1),
                preferred_element_type=jnp.float32,
            )
            summed = summed[:, :head_dim] + summed[:, head_dim:]
            for g in range(group):
                j = h * group + g
                out_ref[:, j * head_dim : (j + 1) * head_dim] = summed[
                    g * rows : (g + 1) * rows
                ].astype(out_ref.dtype)
                here = line == g * rows + row
                best = jnp.sum(jnp.where(here, highest, 0.0), axis=1, keepdims=True)
                sums = jnp.sum(jnp.where(here, total, 0.0), axis=1, keepdims=True)
                all_best = jnp.where(lane == j, best, all_best)
                all_total = jnp.where(lane == j, sums, all_total)
    places, tiles = state_blocks(heads)
    state = [jnp.zeros((rows, LANES), jnp.float32) for _ in range(tiles)]
    for piece, (offset, tile) in zip(in_three(all_best) + in_three(all_total), places):
        state[tile] = state[tile] + pltpu.roll(piece.astype(jnp.float32), offset, 1)
    for tile in range(tiles):
        at = columns + tile * LANES
        out_ref[:, at : at + LANES] = state[tile].astype(out_ref.dtype)


def swap_homes(value, home, peers):
    row = lax.broadcasted_iota(jnp.int32, value.shape, 0)
    mine = lax.axis_index("tensor")
    step = home
    while step < home * peers:
        size = value.shape[0]
        lower = lax.rem(row // step, 2) == 0
        other = jnp.where(
            lower, pltpu.roll(value, size - step, 0), pltpu.roll(value, step, 0)
        )
        value = jnp.where(lax.rem(mine // (step // home), 2) == 1, other, value)
        step *= 2
    return value


def output_kernel(*refs, parts, peers, head_dim):
    part_refs = refs[:parts]
    w_ref = refs[parts]
    out_refs = refs[parts + 1 :]
    rows = part_refs[0].shape[0]
    columns = w_ref.shape[0]
    heads = columns // head_dim
    places, _ = state_blocks(heads)
    bests, totals = [], []
    for ref in part_refs:
        pieces = []
        for offset, tile in places:
            at = columns + tile * LANES
            block = ref[:, at : at + LANES].astype(jnp.float32)
            pieces.append(pltpu.roll(block, (LANES - offset) % LANES, 1))
        bests.append(pieces[0] + pieces[1] + pieces[2])
        totals.append(pieces[3] + pieces[4] + pieces[5])
    highest = functools.reduce(jnp.maximum, bests)
    factors = [jnp.exp(best - highest) for best in bests]
    total = tree_sum([f * t for f, t in zip(factors, totals)])
    shares = [f / total for f in factors]
    pieces = []
    for j in range(heads):
        at = j * head_dim
        pieces.append(
            tree_sum(
                [
                    share[:, j : j + 1] * ref[:, at : at + head_dim].astype(jnp.float32)
                    for share, ref in zip(shares, part_refs)
                ]
            )
        )
    attended = jnp.concatenate(pieces, axis=1)
    home = rows // peers
    attended = swap_homes(attended, home, peers).astype(jnp.bfloat16)
    result = jnp.dot(attended, w_ref[...], preferred_element_type=jnp.float32)
    for i, ref in enumerate(out_refs):
        ref[...] = result[i * home : (i + 1) * home]


def send_all(value, axis):
    size = lax.axis_size(axis)
    if size > DIRECT_MOST:
        gathered = lax.all_gather(value, axis)
        return [gathered[i] for i in range(size)]
    if size & (size - 1) == 0:
        tables = [[(i, i ^ s) for i in range(size)] for s in range(1, size)]
    else:
        tables = [[(i, (i + s) % size) for i in range(size)] for s in range(1, size)]
    return [value] + [lax.ppermute(value, axis, table) for table in tables]


def per_device(
    activations,
    norm_gain,
    w_query,
    w_out,
    key_pool,
    value_block_store,
    block_list,
    block_slot_table,
    kept_len,
):
    rows = activations.shape[0]
    depth, columns = w_query.shape
    kv_heads, slots, tokens, head_dim = key_pool.shape
    group = columns // (kv_heads * head_dim)
    lenders = lax.axis_size("lender")
    peers = lax.axis_size("tensor")
    chunks = max(1, min(4, depth // 256))

    payload = pl.pallas_call(
        project_kernel,
        out_shape=jax.ShapeDtypeStruct((rows, columns + LANES), jnp.float32),
        in_specs=[HBM] * 3,
        out_specs=VMEM,
        scratch_shapes=[
            pltpu.VMEM(activations.shape, activations.dtype),
            pltpu.VMEM((depth // LANES, LANES), norm_gain.dtype),
            pltpu.VMEM((depth, columns), jnp.bfloat16),
            pltpu.SemaphoreType.DMA((2,)),
            pltpu.SemaphoreType.DMA((chunks,)),
        ],
        compiler_params=pltpu.CompilerParams(vmem_limit_bytes=12 << 20),
        name="project",
    )(*in_hbm(activations, norm_gain.reshape(-1, LANES), w_query))

    pick, gather, bias = pl.pallas_call(
        owners_kernel,
        out_shape=(
            jax.ShapeDtypeStruct((kv_heads, slots * group, group * rows), jnp.bfloat16),
            jax.ShapeDtypeStruct((kv_heads, group * rows, slots * group), jnp.bfloat16),
            jax.ShapeDtypeStruct((kv_heads, slots * group, group * rows), jnp.float32),
        ),
        in_specs=[pl.BlockSpec(memory_space=pl.ANY)] + [HBM] * 3,
        out_specs=(VMEM, VMEM, VMEM),
        scratch_shapes=[
            pltpu.VMEM(block_list.shape, block_list.dtype),
            pltpu.VMEM(block_slot_table.shape, block_slot_table.dtype),
            pltpu.VMEM(kept_len.shape[::-1], kept_len.dtype),
            pltpu.SemaphoreType.DMA((3,)),
        ],
        compiler_params=pltpu.CompilerParams(vmem_limit_bytes=8 << 20),
        cost_estimate=pl.CostEstimate(flops=0, bytes_accessed=4 << 20, transcendentals=0),
        name="owners",
    )(payload, *in_hbm(block_list, block_slot_table, kept_len.T))

    if lenders > DIRECT_MOST:
        parts = [lax.psum(payload, "lender")]
    else:
        parts = send_all(payload, "lender")

    tiles = state_blocks(kv_heads * group)[1]
    partial_state = pl.pallas_call(
        functools.partial(attend_kernel, parts=len(parts), width=depth * lenders),
        out_shape=jax.ShapeDtypeStruct((rows, columns + tiles * LANES), jnp.bfloat16),
        in_specs=[VMEM] * (len(parts) + 5),
        out_specs=VMEM,
        compiler_params=pltpu.CompilerParams(vmem_limit_bytes=24 << 20),
        name="attend",
    )(*parts, pick, gather, bias, key_pool, value_block_store)

    parts = send_all(partial_state, "lender")

    home = rows // peers
    sums = pl.pallas_call(
        functools.partial(output_kernel, parts=len(parts), peers=peers, head_dim=head_dim),
        out_shape=[jax.ShapeDtypeStruct((home, w_out.shape[1]), jnp.float32)] * peers,
        in_specs=[VMEM] * (len(parts) + 1),
        out_specs=[VMEM] * peers,
        compiler_params=pltpu.CompilerParams(vmem_limit_bytes=24 << 20),
        name="output",
    )(*parts, w_out)

    result = sums[0]
    for s in range(peers - 1, 0, -1):
        result = result + lax.ppermute(sums[s], "tensor", [(i, i ^ s) for i in range(peers)])
    return result.astype(jnp.bfloat16)


def solution(mesh):
    in_specs = (
        P("group", "lender"),
        P("lender"),
        P("lender", "tensor"),
        P("tensor", "lender"),
        P("tensor", ("group", "lender"), None, None),
        P("tensor", ("group", "lender"), None, None),
        P("group", "tensor", None),
        P("tensor", "group"),
        P("group", "tensor"),
    )
    out_specs = P(("group", "tensor"), "lender")
    return jax.shard_map(
        per_device, mesh=mesh, in_specs=in_specs, out_specs=out_specs, check_vma=False
    )
```

```python
import functools

import jax
import jax.numpy as jnp
from jax import lax
from jax.experimental import pallas as pl
from jax.experimental.pallas import tpu as pltpu
from jax.sharding import PartitionSpec as P

very_low = -1e30
epsilon = 1e-05
LANES = 128
DIRECT_MOST = 8
FIRST_ORDER = (3, 1, 2)
SECOND_ORDER = (1, 2, 3)
VMEM = pl.BlockSpec(memory_space=pltpu.VMEM)
HBM = pl.BlockSpec(memory_space=pltpu.HBM)


def in_three(value):
    pieces = []
    for _ in range(3):
        piece = value.astype(jnp.bfloat16)
        pieces.append(piece)
        value = value - piece.astype(jnp.float32)
    return pieces


def project_kernel(
    act_hbm, gain_hbm, w_hbm, out_ref, act_ref, gain_ref, held, small_sem, sem
):
    depth, columns = w_hbm.shape
    chunks = sem.shape[0]
    step = depth // chunks
    small = [
        pltpu.make_async_copy(act_hbm, act_ref, small_sem.at[0]),
        pltpu.make_async_copy(gain_hbm, gain_ref, small_sem.at[1]),
    ]
    copies = [
        pltpu.make_async_copy(
            w_hbm.at[pl.ds(i * step, step)], held.at[pl.ds(i * step, step)], sem.at[i]
        )
        for i in range(chunks)
    ]
    for copy in small + copies:
        copy.start()
    for copy in small:
        copy.wait()
    rows = act_ref.shape[0]
    features = act_ref[...].astype(jnp.float32)
    squares = jnp.sum(features * features, axis=1, keepdims=True)
    out_ref[:, columns:] = jnp.broadcast_to(squares, (rows, LANES))
    gain = gain_ref[...].astype(jnp.float32)
    gain = jnp.concatenate(
        [jnp.broadcast_to(gain[i : i + 1], (rows, LANES)) for i in range(depth // LANES)], axis=1
    )
    scaled = (features * gain).astype(jnp.bfloat16)
    total = jnp.zeros((rows, columns), jnp.float32)
    for i in range(chunks):
        copies[i].wait()
        total = total + jnp.dot(
            scaled[:, i * step : (i + 1) * step],
            held[i * step : (i + 1) * step, :],
            preferred_element_type=jnp.float32,
        )
    out_ref[:, :columns] = total


def owners_kernel(
    after_hbm, list_hbm, table_hbm, len_hbm, pick_ref, gather_ref, bias_ref,
    list_ref, table_ref, len_ref, sem
):
    pairs = ((list_hbm, list_ref), (table_hbm, table_ref), (len_hbm, len_ref))
    copies = [pltpu.make_async_copy(*pair, sem.at[i]) for i, pair in enumerate(pairs)]
    for copy in copies:
        copy.start()
    for copy in copies:
        copy.wait()
    kv_heads, spots, lines = pick_ref.shape
    rows, _, kept_most = list_ref.shape
    blocks = table_ref.shape[1]
    group = lines // rows
    first_slot = lax.axis_index("lender") * (spots // group)
    logical = lax.broadcasted_iota(jnp.int32, (rows, blocks), 1)
    own_slot = lax.broadcasted_iota(jnp.int32, (spots, blocks), 0) // group + first_slot
    diagonal = lax.broadcasted_iota(jnp.int32, (rows, rows), 0) == lax.broadcasted_iota(
        jnp.int32, (rows, rows), 1
    )
    pick_mask = lax.rem(lax.broadcasted_iota(jnp.int32, (spots, lines), 0), group) == (
        lax.broadcasted_iota(jnp.int32, (spots, lines), 1) // rows
    )
    gather_mask = lax.rem(lax.broadcasted_iota(jnp.int32, (lines, spots), 1), group) == (
        lax.broadcasted_iota(jnp.int32, (lines, spots), 0) // rows
    )
    for h in range(kv_heads):
        listed = list_ref[:, h, :]
        lens = jnp.sum(jnp.where(diagonal, len_ref[h : h + 1, :], 0), axis=1, keepdims=True)
        kept = jnp.zeros((rows, blocks), jnp.float32)
        for k in range(kept_most):
            entry = jnp.where(lens > k, listed[:, k : k + 1], -1)
            kept = jnp.where(entry == logical, 1.0, kept)
        kept = jnp.concatenate([kept] * group, axis=0).astype(jnp.bfloat16)
        placed = jnp.where(own_slot == table_ref[h : h + 1, :], 1.0, 0.0).astype(jnp.bfloat16)
        last = (((1,), (1,)), ((), ()))
        owned = lax.dot_general(placed, kept, last, preferred_element_type=jnp.float32)
        owned = jnp.where(pick_mask, owned, 0.0)
        pick_ref[h] = owned.astype(jnp.bfloat16)
        bias_ref[h] = jnp.where(owned > 0.5, 0.0, very_low)
        owned = lax.dot_general(kept, placed, last, preferred_element_type=jnp.float32)
        gather_ref[h] = jnp.where(gather_mask, owned, 0.0).astype(jnp.bfloat16)


def state_blocks(heads):
    per_tile = max(1, min(6, LANES // heads))
    return [((k % per_tile) * heads, k // per_tile) for k in range(6)], -(-6 // per_tile)


def tree_sum(parts):
    while len(parts) > 1:
        parts = [a + b for a, b in zip(parts[::2], parts[1::2])] + parts[len(parts) & ~1 :]
    return parts[0]


def in_hbm(*arrays):
    return [pltpu.with_memory_space_constraint(a, pltpu.HBM) for a in arrays]


def in_order(refs, order):
    size = len(refs)
    if size > DIRECT_MOST:
        return list(refs)
    order = [s for s in order if s < size] + [s for s in range(1, size) if s not in order]
    by_peer = dict(zip([0] + order, refs))
    return [by_peer[s] for s in range(size)]


def attend_kernel(*refs, parts, width):
    part_refs = in_order(refs[:parts], FIRST_ORDER)
    pick_ref, gather_ref, bias_ref, key_ref, value_ref, out_ref = refs[parts:]
    rows = out_ref.shape[0]
    kv_heads, slots, tokens, head_dim = key_ref.shape
    columns = part_refs[0].shape[1] - LANES
    group = columns // (kv_heads * head_dim)
    heads = kv_heads * group
    lines = group * rows
    both = 2 if kv_heads % 2 == 0 else 1
    some = 2 if slots % 2 == 0 else 1
    square_sum = tree_sum([ref[:, columns:] for ref in part_refs])
    inverse = lax.rsqrt(square_sum / width + epsilon)
    lane = lax.broadcasted_iota(jnp.int32, (rows, LANES), 1)
    line = lax.broadcasted_iota(jnp.int32, (rows, lines), 1)
    row = lax.broadcasted_iota(jnp.int32, (rows, lines), 0)
    all_best = jnp.zeros((rows, LANES), jnp.float32)
    all_total = jnp.zeros((rows, LANES), jnp.float32)
    for first in range(0, kv_heads, both):
        chosen = []
        for i in range(both):
            blocks = []
            for g in range(group):
                at = ((first + i) * group + g) * head_dim
                projected = tree_sum([ref[:, at : at + head_dim] for ref in part_refs])
                blocks.append(projected * inverse * head_dim ** (-0.5))
            query = jnp.concatenate(blocks, axis=0).astype(jnp.bfloat16)
            chosen.append(
                jnp.dot(pick_ref[first + i], query, preferred_element_type=jnp.float32)
            )
        bests = [[] for _ in range(both)]
        totals = [[] for _ in range(both)]
        values = [[] for _ in range(both)]

        def spread(pieces, at, count):
            zero = jnp.zeros_like(pieces[0])
            lined = [
                jnp.concatenate([p if c == where else zero for c in range(count)], axis=1)
                for p, where in zip(pieces, at)
            ]
            return jnp.concatenate(lined, axis=0).astype(jnp.bfloat16)

        def stacked(ref, s):
            return jnp.concatenate(
                [ref[first + i, s : s + some].reshape(some * tokens, head_dim) for i in range(both)],
                axis=1,
            )

        pairs = [(n, i) for n in range(some) for i in range(both)]
        scores, weights = [], []
        for s in range(0, slots, some):
            query = spread(
                [chosen[i][(s + n) * group : (s + n + 1) * group] for n, i in pairs],
                [i for _, i in pairs],
                both,
            )
            score = lax.dot_general(
                query,
                stacked(key_ref, s),
                (((1,), (1,)), ((), ())),
                preferred_element_type=jnp.float32,
            )
            scores += [
                score[at * group : (at + 1) * group, n * tokens : (n + 1) * tokens]
                for at, (n, i) in enumerate(pairs)
            ]
        for at, score in enumerate(scores):
            best = jnp.max(score, axis=1, keepdims=True)
            weight = jnp.exp(score - best)
            i = pairs[at % len(pairs)][1]
            bests[i].append(best)
            totals[i].append(jnp.sum(weight, axis=1, keepdims=True))
            weights.append(weight)
        for s in range(0, slots, some):
            at = s // some * len(pairs)
            summed = jnp.dot(
                spread(weights[at : at + len(pairs)], [n for n, _ in pairs], some),
                stacked(value_ref, s),
                preferred_element_type=jnp.float32,
            )
            for at, (n, i) in enumerate(pairs):
                values[i].append(
                    summed[at * group : (at + 1) * group, i * head_dim : (i + 1) * head_dim]
                )
        for i in range(both):
            h = first + i
            marked = [
                bias_ref[h, s * group : (s + 1) * group, :] + best
                for s, best in enumerate(bests[i])
            ]
            highest = jnp.max(functools.reduce(jnp.maximum, marked), axis=0, keepdims=True)
            against = jnp.maximum(highest, 0.5 * very_low)
            factors = [jnp.exp(m - against) for m in marked]
            total = jnp.sum(
                tree_sum([f * t for f, t in zip(factors, totals[i])]), axis=0, keepdims=True
            )
            scaled = jnp.concatenate(
                [
                    jnp.sum(f, axis=1, keepdims=True) * v
                    for f, v in zip(factors, values[i])
                ],
                axis=0,
            )
            high = scaled.astype(jnp.bfloat16)
            low = (scaled - high.astype(jnp.float32)).astype(jnp.bfloat16)
            summed = jnp.dot(
                gather_ref[h],
                jnp.concatenate([high, low], axis=1),
                preferred_element_type=jnp.float32,
            )
            summed = summed[:, :head_dim] + summed[:, head_dim:]
            for g in range(group):
                j = h * group + g
                out_ref[:, j * head_dim : (j + 1) * head_dim] = summed[
                    g * rows : (g + 1) * rows
                ].astype(out_ref.dtype)
                here = line == g * rows + row
                best = jnp.sum(jnp.where(here, highest, 0.0), axis=1, keepdims=True)
                sums = jnp.sum(jnp.where(here, total, 0.0), axis=1, keepdims=True)
                all_best = jnp.where(lane == j, best, all_best)
                all_total = jnp.where(lane == j, sums, all_total)
    places, tiles = state_blocks(heads)
    state = [jnp.zeros((rows, LANES), jnp.float32) for _ in range(tiles)]
    for piece, (offset, tile) in zip(in_three(all_best) + in_three(all_total), places):
        state[tile] = state[tile] + pltpu.roll(piece.astype(jnp.float32), offset, 1)
    for tile in range(tiles):
        at = columns + tile * LANES
        out_ref[:, at : at + LANES] = state[tile].astype(out_ref.dtype)


def swap_homes(value, home, peers):
    row = lax.broadcasted_iota(jnp.int32, value.shape, 0)
    mine = lax.axis_index("tensor")
    step = home
    while step < home * peers:
        size = value.shape[0]
        lower = lax.rem(row // step, 2) == 0
        other = jnp.where(
            lower, pltpu.roll(value, size - step, 0), pltpu.roll(value, step, 0)
        )
        value = jnp.where(lax.rem(mine // (step // home), 2) == 1, other, value)
        step *= 2
    return value


def output_kernel(*refs, parts, peers, head_dim):
    part_refs = in_order(refs[:parts], SECOND_ORDER)
    w_ref = refs[parts]
    out_refs = refs[parts + 1 :]
    rows = part_refs[0].shape[0]
    columns = w_ref.shape[0]
    heads = columns // head_dim
    places, _ = state_blocks(heads)
    bests, totals = [], []
    for ref in part_refs:
        pieces = []
        for offset, tile in places:
            at = columns + tile * LANES
            block = ref[:, at : at + LANES].astype(jnp.float32)
            pieces.append(pltpu.roll(block, (LANES - offset) % LANES, 1))
        bests.append(pieces[0] + pieces[1] + pieces[2])
        totals.append(pieces[3] + pieces[4] + pieces[5])
    highest = functools.reduce(jnp.maximum, bests)
    factors = [jnp.exp(best - highest) for best in bests]
    total = tree_sum([f * t for f, t in zip(factors, totals)])
    shares = [f / total for f in factors]
    pieces = []
    for j in range(heads):
        at = j * head_dim
        pieces.append(
            tree_sum(
                [
                    share[:, j : j + 1] * ref[:, at : at + head_dim].astype(jnp.float32)
                    for share, ref in zip(shares, part_refs)
                ]
            )
        )
    attended = jnp.concatenate(pieces, axis=1)
    home = rows // peers
    attended = swap_homes(attended, home, peers).astype(jnp.bfloat16)
    result = jnp.dot(attended, w_ref[...], preferred_element_type=jnp.float32)
    for i, ref in enumerate(out_refs):
        ref[...] = result[i * home : (i + 1) * home]


def send_all(value, axis, order):
    size = lax.axis_size(axis)
    if size > DIRECT_MOST:
        gathered = lax.all_gather(value, axis)
        return [gathered[i] for i in range(size)]
    order = [s for s in order if s < size] + [s for s in range(1, size) if s not in order]
    return [value] + [lax.ppermute(value, axis, [(i, i ^ s) for i in range(size)]) for s in order]


def per_device(
    activations,
    norm_gain,
    w_query,
    w_out,
    key_pool,
    value_block_store,
    block_list,
    block_slot_table,
    kept_len,
):
    rows = activations.shape[0]
    depth, columns = w_query.shape
    kv_heads, slots, tokens, head_dim = key_pool.shape
    group = columns // (kv_heads * head_dim)
    lenders = lax.axis_size("lender")
    peers = lax.axis_size("tensor")
    chunks = max(1, min(4, depth // 256))

    payload = pl.pallas_call(
        project_kernel,
        out_shape=jax.ShapeDtypeStruct((rows, columns + LANES), jnp.float32),
        in_specs=[HBM] * 3,
        out_specs=VMEM,
        scratch_shapes=[
            pltpu.VMEM(activations.shape, activations.dtype),
            pltpu.VMEM((depth // LANES, LANES), norm_gain.dtype),
            pltpu.VMEM((depth, columns), jnp.bfloat16),
            pltpu.SemaphoreType.DMA((2,)),
            pltpu.SemaphoreType.DMA((chunks,)),
        ],
        compiler_params=pltpu.CompilerParams(vmem_limit_bytes=12 << 20),
        name="project",
    )(*in_hbm(activations, norm_gain.reshape(-1, LANES), w_query))

    pick, gather, bias = pl.pallas_call(
        owners_kernel,
        out_shape=(
            jax.ShapeDtypeStruct((kv_heads, slots * group, group * rows), jnp.bfloat16),
            jax.ShapeDtypeStruct((kv_heads, group * rows, slots * group), jnp.bfloat16),
            jax.ShapeDtypeStruct((kv_heads, slots * group, group * rows), jnp.float32),
        ),
        in_specs=[pl.BlockSpec(memory_space=pl.ANY)] + [HBM] * 3,
        out_specs=(VMEM, VMEM, VMEM),
        scratch_shapes=[
            pltpu.VMEM(block_list.shape, block_list.dtype),
            pltpu.VMEM(block_slot_table.shape, block_slot_table.dtype),
            pltpu.VMEM(kept_len.shape[::-1], kept_len.dtype),
            pltpu.SemaphoreType.DMA((3,)),
        ],
        compiler_params=pltpu.CompilerParams(vmem_limit_bytes=8 << 20),
        cost_estimate=pl.CostEstimate(flops=0, bytes_accessed=4 << 20, transcendentals=0),
        name="owners",
    )(payload, *in_hbm(block_list, block_slot_table, kept_len.T))

    if lenders > DIRECT_MOST:
        parts = [lax.psum(payload, "lender")]
    else:
        parts = send_all(payload, "lender", FIRST_ORDER)

    tiles = state_blocks(kv_heads * group)[1]
    partial_state = pl.pallas_call(
        functools.partial(attend_kernel, parts=len(parts), width=depth * lenders),
        out_shape=jax.ShapeDtypeStruct((rows, columns + tiles * LANES), jnp.bfloat16),
        in_specs=[VMEM] * (len(parts) + 5),
        out_specs=VMEM,
        compiler_params=pltpu.CompilerParams(
            vmem_limit_bytes=24 << 20
        ),
        name="attend",
    )(*parts, pick, gather, bias, key_pool, value_block_store)

    parts = send_all(partial_state, "lender", SECOND_ORDER)

    home = rows // peers
    sums = pl.pallas_call(
        functools.partial(output_kernel, parts=len(parts), peers=peers, head_dim=head_dim),
        out_shape=[jax.ShapeDtypeStruct((home, w_out.shape[1]), jnp.float32)] * peers,
        in_specs=[VMEM] * (len(parts) + 1),
        out_specs=[VMEM] * peers,
        compiler_params=pltpu.CompilerParams(vmem_limit_bytes=24 << 20),
        name="output",
    )(*parts, w_out)

    result = sums[0]
    for s in range(peers - 1, 0, -1):
        result = result + lax.ppermute(sums[s], "tensor", [(i, i ^ s) for i in range(peers)])
    return result.astype(jnp.bfloat16)


def solution(mesh):
    in_specs = (
        P("group", "lender"),
        P("lender"),
        P("lender", "tensor"),
        P("tensor", "lender"),
        P("tensor", ("group", "lender"), None, None),
        P("tensor", ("group", "lender"), None, None),
        P("group", "tensor", None),
        P("tensor", "group"),
        P("group", "tensor"),
    )
    out_specs = P(("group", "tensor"), "lender")
    return jax.shard_map(
        per_device, mesh=mesh, in_specs=in_specs, out_specs=out_specs, check_vma=False
    )
```

```python
import functools

import jax
import jax.numpy as jnp
from jax import lax
from jax.experimental import pallas as pl
from jax.experimental.pallas import tpu as pltpu
from jax.sharding import PartitionSpec as P

very_low = -1e30
epsilon = 1e-05
LANES = 128
DIRECT_MOST = 8
FIRST_ORDER = (3, 1, 2)
SECOND_ORDER = (1, 2, 3)
VMEM = pl.BlockSpec(memory_space=pltpu.VMEM)
HBM = pl.BlockSpec(memory_space=pltpu.HBM)


def in_three(value):
    pieces = []
    for _ in range(3):
        piece = value.astype(jnp.bfloat16)
        pieces.append(piece)
        value = value - piece.astype(jnp.float32)
    return pieces


def project_kernel(
    act_hbm, gain_hbm, w_hbm, out_ref, act_ref, gain_ref, held, small_sem, sem
):
    depth, columns = w_hbm.shape
    chunks = sem.shape[0]
    step = depth // chunks
    small = [
        pltpu.make_async_copy(act_hbm, act_ref, small_sem.at[0]),
        pltpu.make_async_copy(gain_hbm, gain_ref, small_sem.at[1]),
    ]
    copies = [
        pltpu.make_async_copy(
            w_hbm.at[pl.ds(i * step, step)], held.at[pl.ds(i * step, step)], sem.at[i]
        )
        for i in range(chunks)
    ]
    for copy in small + copies:
        copy.start()
    for copy in small:
        copy.wait()
    rows = act_ref.shape[0]
    features = act_ref[...].astype(jnp.float32)
    squares = jnp.sum(features * features, axis=1, keepdims=True)
    out_ref[:, columns:] = jnp.broadcast_to(squares, (rows, LANES))
    gain = gain_ref[...].astype(jnp.float32)
    gain = jnp.concatenate(
        [jnp.broadcast_to(gain[i : i + 1], (rows, LANES)) for i in range(depth // LANES)], axis=1
    )
    scaled = (features * gain).astype(jnp.bfloat16)
    total = jnp.zeros((rows, columns), jnp.float32)
    for i in range(chunks):
        copies[i].wait()
        total = total + jnp.dot(
            scaled[:, i * step : (i + 1) * step],
            held[i * step : (i + 1) * step, :],
            preferred_element_type=jnp.float32,
        )
    out_ref[:, :columns] = total


def owners_kernel(
    after_hbm, list_hbm, table_hbm, len_hbm, pick_ref, gather_ref, bias_ref,
    list_ref, table_ref, len_ref, sem
):
    pairs = ((list_hbm, list_ref), (table_hbm, table_ref), (len_hbm, len_ref))
    copies = [pltpu.make_async_copy(*pair, sem.at[i]) for i, pair in enumerate(pairs)]
    for copy in copies:
        copy.start()
    for copy in copies:
        copy.wait()
    kv_heads, spots, lines = pick_ref.shape
    rows, _, kept_most = list_ref.shape
    blocks = table_ref.shape[1]
    group = lines // rows
    first_slot = lax.axis_index("lender") * (spots // group)
    logical = lax.broadcasted_iota(jnp.int32, (rows, blocks), 1)
    own_slot = lax.broadcasted_iota(jnp.int32, (spots, blocks), 0) // group + first_slot
    diagonal = lax.broadcasted_iota(jnp.int32, (rows, rows), 0) == lax.broadcasted_iota(
        jnp.int32, (rows, rows), 1
    )
    pick_mask = lax.rem(lax.broadcasted_iota(jnp.int32, (spots, lines), 0), group) == (
        lax.broadcasted_iota(jnp.int32, (spots, lines), 1) // rows
    )
    gather_mask = lax.rem(lax.broadcasted_iota(jnp.int32, (lines, spots), 1), group) == (
        lax.broadcasted_iota(jnp.int32, (lines, spots), 0) // rows
    )
    for h in range(kv_heads):
        listed = list_ref[:, h, :]
        lens = jnp.sum(jnp.where(diagonal, len_ref[h : h + 1, :], 0), axis=1, keepdims=True)
        kept = jnp.zeros((rows, blocks), jnp.float32)
        for k in range(kept_most):
            entry = jnp.where(lens > k, listed[:, k : k + 1], -1)
            kept = jnp.where(entry == logical, 1.0, kept)
        kept = jnp.concatenate([kept] * group, axis=0).astype(jnp.bfloat16)
        placed = jnp.where(own_slot == table_ref[h : h + 1, :], 1.0, 0.0).astype(jnp.bfloat16)
        last = (((1,), (1,)), ((), ()))
        owned = lax.dot_general(placed, kept, last, preferred_element_type=jnp.float32)
        owned = jnp.where(pick_mask, owned, 0.0)
        pick_ref[h] = owned.astype(jnp.bfloat16)
        bias_ref[h] = jnp.where(owned > 0.5, 0.0, very_low)
        owned = lax.dot_general(kept, placed, last, preferred_element_type=jnp.float32)
        gather_ref[h] = jnp.where(gather_mask, owned, 0.0).astype(jnp.bfloat16)


def state_blocks(heads):
    per_tile = max(1, min(6, LANES // heads))
    return [((k % per_tile) * heads, k // per_tile) for k in range(6)], -(-6 // per_tile)


def tree_sum(parts):
    while len(parts) > 1:
        parts = [a + b for a, b in zip(parts[::2], parts[1::2])] + parts[len(parts) & ~1 :]
    return parts[0]


def in_hbm(*arrays):
    return [pltpu.with_memory_space_constraint(a, pltpu.HBM) for a in arrays]


def in_order(refs, order):
    size = len(refs)
    if size > DIRECT_MOST:
        return list(refs)
    order = [s for s in order if s < size] + [s for s in range(1, size) if s not in order]
    by_peer = dict(zip([0] + order, refs))
    return [by_peer[s] for s in range(size)]


def attend_kernel(*refs, parts, width):
    part_refs = in_order(refs[:parts], FIRST_ORDER)
    pick_ref, gather_ref, bias_ref, key_ref, value_ref, out_ref = refs[parts:]
    rows = out_ref.shape[0]
    kv_heads, slots, tokens, head_dim = key_ref.shape
    columns = part_refs[0].shape[1] - LANES
    group = columns // (kv_heads * head_dim)
    heads = kv_heads * group
    lines = group * rows
    both = 2 if kv_heads % 2 == 0 else 1
    some = 2 if slots % 2 == 0 else 1
    square_sum = tree_sum([ref[:, columns:] for ref in part_refs])
    inverse = lax.rsqrt(square_sum / width + epsilon)
    lane = lax.broadcasted_iota(jnp.int32, (rows, LANES), 1)
    line = lax.broadcasted_iota(jnp.int32, (rows, lines), 1)
    row = lax.broadcasted_iota(jnp.int32, (rows, lines), 0)
    all_best = jnp.zeros((rows, LANES), jnp.float32)
    all_total = jnp.zeros((rows, LANES), jnp.float32)
    for first in range(0, kv_heads, both):
        chosen = []
        for i in range(both):
            blocks = []
            for g in range(group):
                at = ((first + i) * group + g) * head_dim
                projected = tree_sum([ref[:, at : at + head_dim] for ref in part_refs])
                blocks.append(projected * inverse * head_dim ** (-0.5))
            query = jnp.concatenate(blocks, axis=0).astype(jnp.bfloat16)
            chosen.append(
                jnp.dot(pick_ref[first + i], query, preferred_element_type=jnp.float32)
            )
        bests = [[] for _ in range(both)]
        totals = [[] for _ in range(both)]
        values = [[] for _ in range(both)]

        def spread(pieces, at, count):
            zero = jnp.zeros_like(pieces[0])
            lined = [
                jnp.concatenate([p if c == where else zero for c in range(count)], axis=1)
                for p, where in zip(pieces, at)
            ]
            return jnp.concatenate(lined, axis=0).astype(jnp.bfloat16)

        def stacked(ref, s):
            return jnp.concatenate(
                [ref[first + i, s : s + some].reshape(some * tokens, head_dim) for i in range(both)],
                axis=1,
            )

        pairs = [(n, i) for n in range(some) for i in range(both)]
        scores, weights = [], []
        for s in range(0, slots, some):
            query = spread(
                [chosen[i][(s + n) * group : (s + n + 1) * group] for n, i in pairs],
                [i for _, i in pairs],
                both,
            )
            score = lax.dot_general(
                query,
                stacked(key_ref, s),
                (((1,), (1,)), ((), ())),
                preferred_element_type=jnp.float32,
            )
            scores += [
                score[at * group : (at + 1) * group, n * tokens : (n + 1) * tokens]
                for at, (n, i) in enumerate(pairs)
            ]
        for at, score in enumerate(scores):
            best = jnp.max(score, axis=1, keepdims=True)
            weight = jnp.exp(score - best)
            i = pairs[at % len(pairs)][1]
            bests[i].append(best)
            totals[i].append(jnp.sum(weight, axis=1, keepdims=True))
            weights.append(weight)
        for s in range(0, slots, some):
            at = s // some * len(pairs)
            summed = jnp.dot(
                spread(weights[at : at + len(pairs)], [n for n, _ in pairs], some),
                stacked(value_ref, s),
                preferred_element_type=jnp.float32,
            )
            for at, (n, i) in enumerate(pairs):
                values[i].append(
                    summed[at * group : (at + 1) * group, i * head_dim : (i + 1) * head_dim]
                )
        for i in range(both):
            h = first + i
            marked = [
                bias_ref[h, s * group : (s + 1) * group, :] + best
                for s, best in enumerate(bests[i])
            ]
            highest = jnp.max(functools.reduce(jnp.maximum, marked), axis=0, keepdims=True)
            against = jnp.maximum(highest, 0.5 * very_low)
            factors = [jnp.exp(m - against) for m in marked]
            total = jnp.sum(
                tree_sum([f * t for f, t in zip(factors, totals[i])]), axis=0, keepdims=True
            )
            scaled = jnp.concatenate(
                [
                    jnp.sum(f, axis=1, keepdims=True) * v
                    for f, v in zip(factors, values[i])
                ],
                axis=0,
            )
            high = scaled.astype(jnp.bfloat16)
            low = (scaled - high.astype(jnp.float32)).astype(jnp.bfloat16)
            summed = jnp.dot(
                gather_ref[h],
                jnp.concatenate([high, low], axis=1),
                preferred_element_type=jnp.float32,
            )
            summed = summed[:, :head_dim] + summed[:, head_dim:]
            for g in range(group):
                j = h * group + g
                out_ref[:, j * head_dim : (j + 1) * head_dim] = summed[
                    g * rows : (g + 1) * rows
                ].astype(out_ref.dtype)
                here = line == g * rows + row
                best = jnp.sum(jnp.where(here, highest, 0.0), axis=1, keepdims=True)
                sums = jnp.sum(jnp.where(here, total, 0.0), axis=1, keepdims=True)
                all_best = jnp.where(lane == j, best, all_best)
                all_total = jnp.where(lane == j, sums, all_total)
    places, tiles = state_blocks(heads)
    state = [jnp.zeros((rows, LANES), jnp.float32) for _ in range(tiles)]
    for piece, (offset, tile) in zip(in_three(all_best) + in_three(all_total), places):
        state[tile] = state[tile] + pltpu.roll(piece.astype(jnp.float32), offset, 1)
    for tile in range(tiles):
        at = columns + tile * LANES
        out_ref[:, at : at + LANES] = state[tile].astype(out_ref.dtype)


def swap_homes(value, home, peers):
    row = lax.broadcasted_iota(jnp.int32, value.shape, 0)
    mine = lax.axis_index("tensor")
    step = home
    while step < home * peers:
        size = value.shape[0]
        lower = lax.rem(row // step, 2) == 0
        other = jnp.where(
            lower, pltpu.roll(value, size - step, 0), pltpu.roll(value, step, 0)
        )
        value = jnp.where(lax.rem(mine // (step // home), 2) == 1, other, value)
        step *= 2
    return value


def output_kernel(*refs, parts, peers, head_dim):
    part_refs = in_order(refs[:parts], SECOND_ORDER)
    w_ref = refs[parts]
    out_refs = refs[parts + 1 :]
    rows = part_refs[0].shape[0]
    columns = w_ref.shape[0]
    heads = columns // head_dim
    places, _ = state_blocks(heads)
    bests, totals = [], []
    for ref in part_refs:
        pieces = []
        for offset, tile in places:
            at = columns + tile * LANES
            block = ref[:, at : at + LANES].astype(jnp.float32)
            pieces.append(pltpu.roll(block, (LANES - offset) % LANES, 1))
        bests.append(pieces[0] + pieces[1] + pieces[2])
        totals.append(pieces[3] + pieces[4] + pieces[5])
    highest = functools.reduce(jnp.maximum, bests)
    factors = [jnp.exp(best - highest) for best in bests]
    total = tree_sum([f * t for f, t in zip(factors, totals)])
    shares = [f / total for f in factors]
    pieces = []
    for j in range(heads):
        at = j * head_dim
        pieces.append(
            tree_sum(
                [
                    share[:, j : j + 1] * ref[:, at : at + head_dim].astype(jnp.float32)
                    for share, ref in zip(shares, part_refs)
                ]
            )
        )
    attended = jnp.concatenate(pieces, axis=1)
    home = rows // peers
    attended = swap_homes(attended, home, peers).astype(jnp.bfloat16)
    result = jnp.dot(attended, w_ref[...], preferred_element_type=jnp.float32)
    for i, ref in enumerate(out_refs):
        ref[...] = result[i * home : (i + 1) * home]


def add_kernel(*refs):
    refs[-1][...] = tree_sum([ref[...] for ref in refs[:-1]]).astype(refs[-1].dtype)


def send_all(value, axis, order):
    size = lax.axis_size(axis)
    if size > DIRECT_MOST:
        gathered = lax.all_gather(value, axis)
        return [gathered[i] for i in range(size)]
    order = [s for s in order if s < size] + [s for s in range(1, size) if s not in order]
    return [value] + [lax.ppermute(value, axis, [(i, i ^ s) for i in range(size)]) for s in order]


def per_device(
    activations,
    norm_gain,
    w_query,
    w_out,
    key_pool,
    value_block_store,
    block_list,
    block_slot_table,
    kept_len,
):
    rows = activations.shape[0]
    depth, columns = w_query.shape
    kv_heads, slots, tokens, head_dim = key_pool.shape
    group = columns // (kv_heads * head_dim)
    lenders = lax.axis_size("lender")
    peers = lax.axis_size("tensor")
    chunks = max(1, min(4, depth // 256))

    payload = pl.pallas_call(
        project_kernel,
        out_shape=jax.ShapeDtypeStruct((rows, columns + LANES), jnp.float32),
        in_specs=[HBM] * 3,
        out_specs=VMEM,
        scratch_shapes=[
            pltpu.VMEM(activations.shape, activations.dtype),
            pltpu.VMEM((depth // LANES, LANES), norm_gain.dtype),
            pltpu.VMEM((depth, columns), jnp.bfloat16),
            pltpu.SemaphoreType.DMA((2,)),
            pltpu.SemaphoreType.DMA((chunks,)),
        ],
        compiler_params=pltpu.CompilerParams(vmem_limit_bytes=12 << 20),
        name="project",
    )(*in_hbm(activations, norm_gain.reshape(-1, LANES), w_query))

    pick, gather, bias = pl.pallas_call(
        owners_kernel,
        out_shape=(
            jax.ShapeDtypeStruct((kv_heads, slots * group, group * rows), jnp.bfloat16),
            jax.ShapeDtypeStruct((kv_heads, group * rows, slots * group), jnp.bfloat16),
            jax.ShapeDtypeStruct((kv_heads, slots * group, group * rows), jnp.float32),
        ),
        in_specs=[pl.BlockSpec(memory_space=pl.ANY)] + [HBM] * 3,
        out_specs=(VMEM, VMEM, VMEM),
        scratch_shapes=[
            pltpu.VMEM(block_list.shape, block_list.dtype),
            pltpu.VMEM(block_slot_table.shape, block_slot_table.dtype),
            pltpu.VMEM(kept_len.shape[::-1], kept_len.dtype),
            pltpu.SemaphoreType.DMA((3,)),
        ],
        compiler_params=pltpu.CompilerParams(vmem_limit_bytes=8 << 20),
        cost_estimate=pl.CostEstimate(flops=0, bytes_accessed=4 << 20, transcendentals=0),
        name="owners",
    )(payload, *in_hbm(block_list, block_slot_table, kept_len.T))

    if lenders > DIRECT_MOST:
        parts = [lax.psum(payload, "lender")]
    else:
        parts = send_all(payload, "lender", FIRST_ORDER)

    tiles = state_blocks(kv_heads * group)[1]
    partial_state = pl.pallas_call(
        functools.partial(attend_kernel, parts=len(parts), width=depth * lenders),
        out_shape=jax.ShapeDtypeStruct((rows, columns + tiles * LANES), jnp.bfloat16),
        in_specs=[VMEM] * (len(parts) + 5),
        out_specs=VMEM,
        compiler_params=pltpu.CompilerParams(
            vmem_limit_bytes=24 << 20
        ),
        name="attend",
    )(*parts, pick, gather, bias, key_pool, value_block_store)

    parts = send_all(partial_state, "lender", SECOND_ORDER)

    home = rows // peers
    sums = pl.pallas_call(
        functools.partial(output_kernel, parts=len(parts), peers=peers, head_dim=head_dim),
        out_shape=[jax.ShapeDtypeStruct((home, w_out.shape[1]), jnp.float32)] * peers,
        in_specs=[VMEM] * (len(parts) + 1),
        out_specs=[VMEM] * peers,
        compiler_params=pltpu.CompilerParams(vmem_limit_bytes=24 << 20),
        name="output",
    )(*parts, w_out)

    came = [sums[0]] + [
        lax.ppermute(sums[s], "tensor", [(i, i ^ s) for i in range(peers)])
        for s in range(peers - 1, 0, -1)
    ]
    return pl.pallas_call(
        add_kernel,
        out_shape=jax.ShapeDtypeStruct(sums[0].shape, jnp.bfloat16),
        in_specs=[VMEM] * peers,
        out_specs=VMEM,
        compiler_params=pltpu.CompilerParams(vmem_limit_bytes=2 << 20),
        name="add",
    )(*came)


def solution(mesh):
    in_specs = (
        P("group", "lender"),
        P("lender"),
        P("lender", "tensor"),
        P("tensor", "lender"),
        P("tensor", ("group", "lender"), None, None),
        P("tensor", ("group", "lender"), None, None),
        P("group", "tensor", None),
        P("tensor", "group"),
        P("group", "tensor"),
    )
    out_specs = P(("group", "tensor"), "lender")
    return jax.shard_map(
        per_device, mesh=mesh, in_specs=in_specs, out_specs=out_specs, check_vma=False
    )
```
